128 devices in a mesh: row: 8 (over x, core), col: 16 (over z, y).
Axes of the slice: x: 4, y: 4, z: 4, core: 2. Of those that a mesh axis runs over, the one named last changes fastest.
Arguments:
- features: float32 [32768, 128], P('col', 'row'), may hold values from -6 to 6
- tile_rows: int32 [8, 16, 80], P('row', 'col'), may hold values from 0 to 32, as said below
- tile_cols: int32 [8, 16, 80], P('row', 'col'), may hold values from 0 to 15
- tile_values: float32 [8, 16, 80, 128, 128], P('row', 'col'), may hold values from -0.51881118 to 0.51881118, as said below
- weight_in: float32 [128, 256], replicated, may hold values from -0.5 to 0.5
- weight_out: float32 [256, 256], replicated, may hold values from -0.375 to 0.375
- cotangent: float32 [32768, 256], P(('col', 'row')), may hold values from -0.03125 to 0.03125
Outputs:
- output: float32 [32768, 256], P(('col', 'row'))
- grad_in: float32 [128, 256], replicated
- grad_out: float32 [256, 256], replicated
The draws below stay inside these ranges and needn't reach their ends.
Inputs may be any that keep to these rules, and one draw needn't show every extreme that they name: `tile_rows`: slot s of device (i, j) is used for s below that device's tile count and holds a tile row 0 to 31; unused slots hold 32. Used slots come first, no (row, column) pair repeats within a device, and in every draw some device uses all 80 slots. `tile_values`: A tile is sparse: each entry is nonzero with probability 2.56 / 128, at random positions.
All inputs are finite; a program needn't handle non-finite values.
Results may differ from the reference program's by a relative error of at most 0.0003.
Values sent between devices are 32-bit elements; how exact they have to be, the bound alone decides.
A program may use at most 128 MiB of HBM per device.

```python
import math
import jax
import jax.numpy as jnp
from jax import lax

F_IN = 128
UNITS = 256
TILE = 128
ROWS_DEV = 256
TILES_DEV = 80
NODES = 32768
TROWS = 32
TCOLS = 16
N_ROW = 8
N_COL = 16


def tile_layout(key):
    base_key = jax.random.fold_in(key, 11)
    devices_all = N_ROW * N_COL
    positions = TROWS * TCOLS
    dev_keys = jax.random.split(base_key, devices_all)
    shuffled = jax.vmap(lambda k: jax.random.permutation(k, positions))(dev_keys)
    shuffled = shuffled[:, :TILES_DEV].astype(jnp.int32)
    fewest = TILES_DEV // 8
    uniform_ints = jax.random.randint(jax.random.fold_in(base_key, 1), (devices_all,), 0, 1024).astype(jnp.int32)
    counts = fewest + (TILES_DEV - fewest) * uniform_ints * uniform_ints // (1024 * 1024)
    busiest = jax.random.randint(jax.random.fold_in(base_key, 2), (), 0, devices_all).astype(jnp.int32)
    counts = jnp.where(jnp.arange(devices_all, dtype=jnp.int32) == busiest, TILES_DEV, counts)
    in_use = jnp.arange(TILES_DEV, dtype=jnp.int32)[None, :] < counts[:, None]
    tile_row = jnp.where(in_use, shuffled // TCOLS, TROWS).astype(jnp.int32)
    tile_col = (shuffled % TCOLS).astype(jnp.int32)
    return (tile_row.reshape(N_ROW, N_COL, TILES_DEV), tile_col.reshape(N_ROW, N_COL, TILES_DEV))


def draw_tile_rows(key, part):
    return tile_layout(key)[0]


def draw_tile_cols(key, part):
    return tile_layout(key)[1]


def draw_tile_values(key, part):
    value_key = jax.random.fold_in(key, 23)
    shape = (N_ROW, N_COL, TILES_DEV, TILE, TILE)
    density = 2.56 / TILE
    spread = 1.5 * math.sqrt(ROWS_DEV / (2.56 * TILES_DEV * TILE))
    nonzero = jax.random.bernoulli(jax.random.fold_in(value_key, 1), density, shape)
    raw_values = jnp.clip(jax.random.normal(jax.random.fold_in(value_key, 2), shape, jnp.float32), -3.5, 3.5)
    return jnp.where(nonzero, raw_values * spread, 0.0).astype(jnp.float32)


def shard_levels(rng, shape, cuts, smallest, top_value):
    loudness, own = 1.0, jax.random.fold_in(rng, 6)
    for position, shards_of in cuts:
        draws = jnp.exp(jax.random.uniform(jax.random.fold_in(own, position), (shards_of,), jnp.float32, smallest / len(cuts), top_value / len(cuts)))
        loudness = loudness * jnp.repeat(draws, shape[position] // shards_of).reshape([-1 if axis == position else 1 for axis in range(len(shape))])
    return loudness


def centred(stream_key, extent, scale, bound, cuts=(), kind=jnp.bfloat16):
    result = scale * jax.random.normal(stream_key, extent, jnp.float32)
    if cuts:
        result = result * shard_levels(stream_key, extent, cuts, -0.22, 0.18)
    return jnp.clip(result, -bound, bound).astype(kind)


def setup_inputs(seed: int = 0) -> dict:
    keys = jax.random.split(jax.random.key(seed), 8)
    return {
        "features": centred(keys[0], (NODES, F_IN), 1.0, 6.0, ((0, 16), (1, 8)), jnp.float32),
        "tile_rows": draw_tile_rows(jax.random.fold_in(keys[7], 71), 0),
        "tile_cols": draw_tile_cols(jax.random.fold_in(keys[7], 71), 0),
        "tile_values": draw_tile_values(jax.random.fold_in(keys[7], 71), 0),
        "weight_in": centred(keys[4], (F_IN, UNITS), F_IN ** -0.5, 0.5, (), jnp.float32),
        "weight_out": centred(keys[5], (UNITS, UNITS), UNITS ** -0.5, 0.375, (), jnp.float32),
        "cotangent": centred(keys[6], (NODES, UNITS), NODES ** -0.5, 0.03125, ((0, 128),), jnp.float32),
    }


def apply_forward(support, tile_rows, tile_cols, tile_values):
    width = support.shape[1]
    col_blocks = support.reshape(N_COL, TCOLS, TILE, width)

    def per_block_row(row_index):
        def add_device(running, col_index):
            tile_row = tile_rows[row_index, col_index]
            tile_col = tile_cols[row_index, col_index]
            tile_block = tile_values[row_index, col_index]
            picked = col_blocks[col_index][tile_col]
            products = jnp.einsum('tab,tbf->taf', tile_block, picked, precision=lax.Precision.HIGHEST)
            summed = jax.ops.segment_sum(products, tile_row, num_segments=TROWS + 1)[:TROWS]
            return running + summed, None

        start = jnp.zeros((TROWS, TILE, width), jnp.float32)
        running, _ = lax.scan(add_device, start, jnp.arange(N_COL, dtype=jnp.int32))
        return running.reshape(N_COL, ROWS_DEV, width)

    blocks = lax.map(per_block_row, jnp.arange(N_ROW, dtype=jnp.int32))
    return jnp.transpose(blocks, (1, 0, 2, 3)).reshape(NODES, width)


def apply_adjoint(grads, tile_rows, tile_cols, tile_values):
    width = grads.shape[1]
    grid_rows = grads.reshape(N_COL, N_ROW, ROWS_DEV, width)

    def per_block_col(col_index):
        def add_device(running, row_index):
            tile_row = tile_rows[row_index, col_index]
            tile_col = tile_cols[row_index, col_index]
            tile_block = tile_values[row_index, col_index]
            row_block = grid_rows[:, row_index].reshape(TROWS, TILE, width)
            picked = row_block[jnp.minimum(tile_row, TROWS - 1)]
            products = jnp.einsum('tba,tbf->taf', tile_block, picked, precision=lax.Precision.HIGHEST)
            target = jnp.where(tile_row < TROWS, tile_col, TCOLS)
            summed = jax.ops.segment_sum(products, target, num_segments=TCOLS + 1)[:TCOLS]
            return running + summed, None

        start = jnp.zeros((TCOLS, TILE, width), jnp.float32)
        running, _ = lax.scan(add_device, start, jnp.arange(N_ROW, dtype=jnp.int32))
        return running.reshape(N_ROW * ROWS_DEV, width)

    blocks = lax.map(per_block_col, jnp.arange(N_COL, dtype=jnp.int32))
    return blocks.reshape(NODES, width)


def reference(features, tile_rows, tile_cols, tile_values, weight_in, weight_out, cotangent):
    highest = lax.Precision.HIGHEST
    support = jnp.dot(features, weight_in, precision=highest, preferred_element_type=jnp.float32)
    pre_act = apply_forward(support, tile_rows, tile_cols, tile_values)
    hidden = jax.nn.silu(pre_act)
    support_two = jnp.dot(hidden, weight_out, precision=highest, preferred_element_type=jnp.float32)
    output = apply_forward(support_two, tile_rows, tile_cols, tile_values)
    d_support_two = apply_adjoint(cotangent, tile_rows, tile_cols, tile_values)
    grad_out = jnp.dot(hidden.T, d_support_two, precision=highest, preferred_element_type=jnp.float32)
    d_hidden = jnp.dot(d_support_two, weight_out.T, precision=highest, preferred_element_type=jnp.float32)
    sigmoid_pre = jax.nn.sigmoid(pre_act)
    d_pre = d_hidden * sigmoid_pre * (1.0 + pre_act * (1.0 - sigmoid_pre))
    d_support = apply_adjoint(d_pre, tile_rows, tile_cols, tile_values)
    grad_in = jnp.dot(features.T, d_support, precision=highest, preferred_element_type=jnp.float32)
    return (output, grad_in, grad_out)
```

```python
import functools

import jax
import jax.numpy as jnp
from jax import lax
from jax.experimental import pallas as pl
from jax.experimental.pallas import tpu as pltpu
from jax.sharding import PartitionSpec as P

MESH = pl.DeviceIdType.MESH
F32 = jnp.float32
BF16 = jnp.bfloat16
VMEM_LIMIT = 60 * 1024 * 1024
CHUNK = 8


def split(v):
    hi = v.astype(BF16)
    return hi, (v - hi.astype(F32)).astype(BF16)


def dot16(a, b, dims=(((1,), (0,)), ((), ()))):
    return lax.dot_general(a, b, dims, preferred_element_type=F32)


def dot3(a, b, dims=(((1,), (0,)), ((), ()))):
    ah, al = split(a)
    bh, bl = split(b)
    return dot16(ah, bl, dims) + dot16(al, bh, dims) + dot16(ah, bh, dims)


class Net:
    def __init__(self, send_sems, recv_sems):
        self.send_sems, self.recv_sems = send_sems, recv_sems
        self.copies = []
        i, j = lax.axis_index("row"), lax.axis_index("col")
        self.x, self.core = i // 2, lax.rem(i, 2)
        self.z, self.y = j // 4, lax.rem(j, 4)
        self.i, self.j = i, j
        self.queue = []

    def pos(self, axis):
        return {"x": self.x, "y": self.y, "z": self.z}[axis]

    def at(self, axis, shift):
        return lax.rem(self.pos(axis) + (shift + 4), 4)

    def peer(self, axis, shift):
        if axis == "core":
            return (self.x * 2 + 1 - self.core, self.j)
        p = self.at(axis, shift)
        if axis == "x":
            return (p * 2 + self.core, self.j)
        if axis == "y":
            return (self.i, self.z * 4 + p)
        return (self.i, p * 4 + self.y)

    def barrier(self, axes):
        sem = pltpu.get_barrier_semaphore()
        n = 0
        for axis in axes:
            for shift in (1,) if axis == "core" else (1, -1):
                pl.semaphore_signal(sem, inc=1, device_id=self.peer(axis, shift), device_id_type=MESH)
                n += 1
        pl.semaphore_wait(sem, n)

    def send(self, src, dst, axis, shift=1):
        k = len(self.copies)
        copy = pltpu.make_async_remote_copy(
            src_ref=src,
            dst_ref=dst,
            send_sem=self.send_sems.at[k],
            recv_sem=self.recv_sems.at[k],
            device_id=self.peer(axis, shift),
            device_id_type=MESH,
        )
        copy.start()
        self.copies.append(copy)
        return copy

    def spawn(self, gen):
        self.queue.append(gen)

    def run(self):
        while self.queue:
            gen = self.queue.pop(0)
            try:
                next(gen)
            except StopIteration:
                continue
            self.queue.append(gen)
        for copy in self.copies:
            copy.wait_send()


def ag_ring(net, axis, src, ref, have, units=2):
    p, up, down, far = net.at(axis, 0), net.at(axis, 1), net.at(axis, -1), net.at(axis, 2)
    last = units - 1
    plus, minus = {}, {}
    for u in range(units):
        plus[u] = net.send(src(u), ref(p, u), axis, 1)
        v = last - u
        minus[v] = net.send(src(v), ref(p, v), axis, -1)
    yield
    plus[0].wait_recv()
    f0 = net.send(ref(down, 0), ref(down, 0), axis, 1)
    f1 = None
    if units == 2:
        minus[1].wait_recv()
        f1 = net.send(ref(up, 1), ref(up, 1), axis, -1)
    yield
    if units == 2:
        plus[1].wait_recv()
    have(down)
    minus[0].wait_recv()
    have(up)
    yield
    f0.wait_recv()
    if f1 is not None:
        f1.wait_recv()
    have(far)


def rs_ring(net, axis, part, ready, stage, emit, units=2):
    p, up, down, far = net.at(axis, 0), net.at(axis, 1), net.at(axis, -1), net.at(axis, 2)
    r0, r1, m0, m1, q0, q1 = (stage(k) for k in range(6))
    while not ready[2]:
        yield
    a0 = net.send(part(far, 0), r0, axis, 1)
    a1 = net.send(part(far, 1), r1, axis, -1) if units == 2 else None
    while not (ready[1] and ready[-1]):
        yield
    b0 = net.send(part(down, 0), q0, axis, -1)
    b1 = net.send(part(up, 1), m1, axis, 1) if units == 2 else None
    yield
    a0.wait_recv()
    r0[...] = r0[...] + part(up, 0)[...]
    c0 = net.send(r0, m0, axis, 1)
    if units == 2:
        a1.wait_recv()
        r1[...] = r1[...] + part(down, 1)[...]
        c1 = net.send(r1, q1, axis, -1)
    while not ready[0]:
        yield
    yield
    b0.wait_recv()
    c0.wait_recv()
    emit(0, part(p, 0)[...] + (m0[...] + q0[...]))
    if units == 2:
        b1.wait_recv()
        c1.wait_recv()
        emit(1, part(p, 1)[...] + (m1[...] + q1[...]))


ALL = {0: True, 1: True, 2: True, -1: True}
SHIFTS = (2, 1, -1, 0)


def rs_plane(net, tiles, stage_one, middle, stage_two, out, done):
    for part, (first, second) in enumerate((("z", "y"), ("y", "z"))):
        ready = {d: False for d in SHIFTS}

        def block(a, b, first=first):
            return a * 4 + b if first == "z" else b * 4 + a

        for k, d in enumerate(SHIFTS):
            pos2 = net.at(second, d)
            left = [2]

            def term(pos1, u, pos2=pos2, part=part, block=block):
                return tiles.at[2 * block(pos1, pos2) + part, pl.ds(u * 64, 64), :]

            def land(s, part=part, k=k):
                return stage_one.at[part, k, s]

            def emit(u, value, part=part, pos2=pos2, d=d, left=left, ready=ready):
                middle[part, pos2, u] = value
                left[0] -= 1
                if left[0] == 0:
                    ready[d] = True

            net.spawn(rs_ring(net, first, term, ALL, land, emit))

        def term2(pos, u, part=part):
            return middle.at[part, pos, u]

        def land2(s, part=part):
            return stage_two.at[part, s]

        def emit2(u, value, part=part):
            out[pl.ds(part * 128 + u * 64, 64), :] = value
            done.append((part, u))

        net.spawn(rs_ring(net, second, term2, ready, land2, emit2))


def gather_kernel(feat_ref, cot_ref, xt_ref, cots_ref, send_sems, recv_sems, local_sems):
    net = Net(send_sems, recv_sems)
    net.barrier(("x", "core", "y", "z"))
    own = [
        pltpu.make_async_copy(feat_ref, xt_ref.at[net.i], local_sems.at[0]),
        pltpu.make_async_copy(cot_ref, cots_ref.at[net.j], local_sems.at[1]),
    ]
    for copy in own:
        copy.start()
    sibling = []

    def row_src(u):
        return feat_ref.at[pl.ds(u * 8, 8), :]

    def row_ref(pos, u):
        return xt_ref.at[pos * 2 + net.core, pl.ds(u * 8, 8), :]

    def row_have(pos):
        block = xt_ref.at[pos * 2 + net.core]
        sibling.append(net.send(block, block, "core"))

    sibling.append(net.send(feat_ref, xt_ref.at[net.i], "core"))
    net.spawn(ag_ring(net, "x", row_src, row_ref, row_have))

    for part, (first, second) in enumerate((("y", "z"), ("z", "y"))):

        def block(a, b, first=first):
            return a + b * 4 if first == "y" else a * 4 + b

        def rows(u, part=part):
            return pl.ds(part * 128 + u * 64, 64)

        def start_second(pos1, src, part=part, second=second, block=block, rows=rows):
            def ref(pos2, u):
                return cots_ref.at[block(pos1, pos2), rows(u), :]

            net.spawn(ag_ring(net, second, src, ref, lambda pos: None))

        def own_src(u, rows=rows):
            return cot_ref.at[rows(u), :]

        def ref_one(pos1, u, second=second, block=block, rows=rows):
            return cots_ref.at[block(pos1, net.at(second, 0)), rows(u), :]

        def have_one(pos1, start_second=start_second, ref_one=ref_one):
            start_second(pos1, lambda u: ref_one(pos1, u))

        net.spawn(ag_ring(net, first, own_src, ref_one, have_one))
        start_second(net.at(first, 0), own_src)
    net.run()
    for copy in sibling:
        copy.wait_recv()
    for copy in own:
        copy.wait()


def tile_copies(tiles_ref, buf, sems):
    n = tiles_ref.shape[0] // CHUNK
    return [
        pltpu.make_async_copy(tiles_ref.at[pl.ds(k * CHUNK, CHUNK)], buf.at[pl.ds(k * CHUNK, CHUNK)], sems.at[k])
        for k in range(n)
    ]


def wait_chunk(tiles_ref, buf, sems, k):
    rows = pl.ds(k * CHUNK, CHUNK)
    pltpu.make_async_copy(tiles_ref.at[rows], buf.at[rows], sems.at[k]).wait()


def first_products_kernel(rows_ref, cols_ref, tiles_ref, xt_ref, cots_ref, fwd_ref, adj_ref,
                          buf, cbuf, xh, xl, ch, cl, sems, csem):
    copies = tile_copies(tiles_ref, buf, sems)
    for copy in copies:
        copy.start()
    ccopy = pltpu.make_async_copy(cots_ref, cbuf, csem)
    ccopy.start()
    fwd_ref[...] = jnp.zeros_like(fwd_ref)
    adj_ref[...] = jnp.zeros_like(adj_ref)

    def split_x(c, _):
        h, l = split(jnp.transpose(xt_ref[:, pl.ds(pl.multiple_of(c * 128, 128), 128)]))
        xh[c] = h
        xl[c] = l
        return 0

    lax.fori_loop(0, 16, split_x, 0)

    def fwd(k, _):
        wait_chunk(tiles_ref, buf, sems, k)
        for s in range(CHUNK):
            t = k * CHUNK + s
            r, c = rows_ref[t], cols_ref[t]
            h, l = split(buf[t])
            w = jnp.concatenate([xh[c], xl[c]], axis=1)
            res = dot16(jnp.concatenate([h, l], axis=1), jnp.concatenate([w, w], axis=0))
            fwd_ref[r] += res[:, :128] + res[:, 128:]
        return 0

    lax.fori_loop(0, len(copies), fwd, 0)
    ccopy.wait()

    def split_c(r, _):
        h, l = split(cbuf[r])
        ch[r] = h
        cl[r] = l
        return 0

    lax.fori_loop(0, 32, split_c, 0)

    def adj(k, _):
        for s in range(CHUNK):
            t = k * CHUNK + s
            r, c = rows_ref[t], cols_ref[t]
            target = jnp.where(r < 32, c, 16)
            r = jnp.minimum(r, 31)
            h, l = split(jnp.transpose(buf[t]))
            w = ch[r]
            res = dot16(jnp.concatenate([h, l], axis=1), jnp.concatenate([w, w], axis=0))
            adj_ref[target] += res + dot16(h, cl[r])
        return 0

    lax.fori_loop(0, len(copies), adj, 0)


def second_product_kernel(rows_ref, cols_ref, tiles_ref, s_ref, fwd_ref, buf, xh, xl, sems):
    copies = tile_copies(tiles_ref, buf, sems)
    for copy in copies:
        copy.start()
    fwd_ref[...] = jnp.zeros_like(fwd_ref)

    def split_x(c, _):
        h, l = split(s_ref[c])
        xh[c] = h
        xl[c] = l
        return 0

    lax.fori_loop(0, 16, split_x, 0)

    def fwd(k, _):
        wait_chunk(tiles_ref, buf, sems, k)
        for s in range(CHUNK):
            t = k * CHUNK + s
            r, c = rows_ref[t], cols_ref[t]
            h, l = split(buf[t])
            w = xh[c]
            res = dot16(jnp.concatenate([h, l], axis=1), jnp.concatenate([w, w], axis=0))
            fwd_ref[r] += res + dot16(h, xl[c])
        return 0

    lax.fori_loop(0, len(copies), fwd, 0)


def middle_kernel(fwd_ref, adj_ref, win_ref, wout_ref, s2_ref, g_ref,
                  stage_a, mid_a, stage_b, s_buf, stage_c, mid_c, stage_d, d_buf, h_buf, p_buf, s2_buf,
                  g_buf, stage_e, g_one, stage_f, g_two, stage_g, send_sems, recv_sems, local_sem):
    net = Net(send_sems, recv_sems)
    net.barrier(("x", "core", "y", "z"))
    done_s, done_d, sibling = [], [], []
    rs_plane(net, fwd_ref, stage_a, mid_a, stage_b, s_buf, done_s)

    ready = {d: False for d in SHIFTS}

    def cores():
        copies = []
        for k, d in enumerate(SHIFTS):
            block = net.at("x", d) * 2 + 1 - net.core
            copies.append(net.send(adj_ref.at[pl.ds(block * 2, 2)], stage_c.at[k], "core"))
        yield
        for k, d in enumerate(SHIFTS):
            copies[k].wait_recv()
            pos = net.at("x", d)
            mid_c[pos] = adj_ref[pl.ds((pos * 2 + net.core) * 2, 2)] + stage_c[k]
            ready[d] = True
            yield

    def emit_d(u, value):
        d_buf[pl.ds(u * 128, 128), :] = value
        done_d.append(u)

    net.spawn(cores())
    net.spawn(rs_ring(net, "x", lambda pos, u: mid_c.at[pos, u], ready, lambda s: stage_d.at[s], emit_d))
    local = pltpu.make_async_copy(s2_buf, s2_ref.at[net.i], local_sem)

    def s2_have(pos):
        block = s2_ref.at[pos * 2 + net.core]
        sibling.append(net.send(block, block, "core"))

    def dense():
        while len(done_s) < 4:
            yield
        pre = dot3(s_buf[...], win_ref[...])
        hidden = pre * (1.0 / (1.0 + jnp.exp(-pre)))
        p_buf[...] = pre
        h_buf[...] = hidden
        s2_buf[...] = dot3(hidden, wout_ref[...]).reshape(2, 128, 256)
        local.start()
        sibling.append(net.send(s2_buf, s2_ref.at[net.i], "core"))
        net.spawn(ag_ring(net, "x", lambda u: s2_buf.at[u], lambda pos, u: s2_ref.at[pos * 2 + net.core, u], s2_have))
        while len(done_d) < 2:
            yield
        d = d_buf[...]
        pre = p_buf[...]
        sg = 1.0 / (1.0 + jnp.exp(-pre))
        d_pre = dot3(d, wout_ref[...], (((1,), (1,)), ((), ()))) * sg * (1.0 + pre * (1.0 - sg))
        grad_in = dot3(jnp.transpose(s_buf[...]), d_pre)
        grad_out = dot3(jnp.transpose(h_buf[...]), d)
        for c in range(2):
            lanes = slice(c * 128, c * 128 + 128)
            g_buf[c, pl.ds(0, 128), :] = grad_in[:, lanes]
            g_buf[c, pl.ds(128, 256), :] = grad_out[:, lanes]
        swap = net.send(g_buf.at[1 - net.core], stage_e, "core")
        yield
        swap.wait_recv()
        g_one[...] = (g_buf[net.core] + stage_e[...]).reshape(g_one.shape)
        one, two = [], []

        def emit_one(u, value):
            g_two[...] = value.reshape(g_two.shape)
            one.append(u)

        net.spawn(rs_ring(net, "y", lambda pos, u: g_one.at[pos], ALL, lambda s: stage_f.at[s], emit_one, units=1))
        while not one:
            yield

        def emit_two(u, value):
            g_ref[...] = value
            two.append(u)

        net.spawn(rs_ring(net, "z", lambda pos, u: g_two.at[pos], ALL, lambda s: stage_g.at[s], emit_two, units=1))

    net.spawn(dense())
    net.run()
    for copy in sibling:
        copy.wait_recv()
    local.wait()


def last_kernel(fwd_ref, g_ref, out_ref, gin_ref, gout_ref,
                stage_a, mid_a, stage_b, gx, gz, gy, gsib, send_sems, recv_sems):
    net = Net(send_sems, recv_sems)
    net.barrier(("x", "core", "y", "z"))
    done = []

    def grads():
        def walk(axis, src, dst):
            got = []
            net.spawn(ag_ring(net, axis, lambda u: src, lambda pos, u: dst.at[pos], got.append, units=1))
            while len(got) < 3:
                yield

        gx[net.x] = g_ref[...]
        yield from walk("x", g_ref, gx)
        gz[net.z] = (gx[0] + gx[1]) + (gx[2] + gx[3])
        yield from walk("z", gz.at[net.z], gz)
        gy[net.y] = gz[...].reshape(96, 128)
        yield from walk("y", gy.at[net.y], gy)
        swap = net.send(gy, gsib, "core")
        yield
        swap.wait_recv()
        mine, other = gy[...].reshape(384, 128), gsib[...].reshape(384, 128)
        first = net.core == 0
        low = jnp.where(first, mine, other)
        high = jnp.where(first, other, mine)
        gin_ref[:, :128] = low[:128]
        gin_ref[:, 128:] = high[:128]
        gout_ref[:, :128] = low[128:]
        gout_ref[:, 128:] = high[128:]

    net.spawn(grads())
    rs_plane(net, fwd_ref, stage_a, mid_a, stage_b, out_ref, done)
    net.run()


ANY = pl.BlockSpec(memory_space=pl.ANY)
VM = pl.BlockSpec(memory_space=pltpu.VMEM)
SM = pl.BlockSpec(memory_space=pltpu.SMEM)


def params(collective_id=None):
    return pltpu.CompilerParams(
        collective_id=collective_id,
        has_side_effects=collective_id is not None,
        vmem_limit_bytes=VMEM_LIMIT,
    )


def sems(n):
    return [pltpu.SemaphoreType.DMA((n,)), pltpu.SemaphoreType.DMA((n,))]


def plane_scratch(width):
    return [
        pltpu.VMEM((2, 4, 6, 64, width), F32),
        pltpu.VMEM((2, 4, 2, 64, width), F32),
        pltpu.VMEM((2, 6, 64, width), F32),
    ]


def shape(*dims):
    return jax.ShapeDtypeStruct(dims, F32)


def per_device(features, tile_rows, tile_cols, tile_values, weight_in, weight_out, cotangent):
    slots = tile_rows.shape[-1]
    rows, cols = tile_rows.reshape(slots), tile_cols.reshape(slots)
    tiles = tile_values.reshape(slots, 128, 128)

    xt, cots = pl.pallas_call(
        gather_kernel,
        out_shape=(shape(8, 16, 2048), shape(16, 256, 256)),
        in_specs=[ANY, ANY],
        out_specs=(ANY, ANY),
        scratch_shapes=sems(80) + [pltpu.SemaphoreType.DMA((2,))],
        compiler_params=params(0),
        name="gather",
    )(features.T, cotangent)

    fwd, adj = pl.pallas_call(
        first_products_kernel,
        out_shape=(shape(33, 128, 128), shape(17, 128, 256)),
        in_specs=[SM, SM, ANY, VM, ANY],
        out_specs=(VM, VM),
        scratch_shapes=[
            pltpu.VMEM((slots, 128, 128), F32),
            pltpu.VMEM((32, 128, 256), F32),
            pltpu.VMEM((16, 128, 128), BF16),
            pltpu.VMEM((16, 128, 128), BF16),
            pltpu.VMEM((32, 128, 256), BF16),
            pltpu.VMEM((32, 128, 256), BF16),
            pltpu.SemaphoreType.DMA((slots // CHUNK,)),
            pltpu.SemaphoreType.DMA,
        ],
        compiler_params=params(),
        name="first_products",
    )(rows, cols, tiles, xt.reshape(128, 2048), cots.reshape(32, 128, 256))

    s2, g = pl.pallas_call(
        middle_kernel,
        out_shape=(shape(8, 2, 128, 256), shape(24, 128)),
        in_specs=[VM, VM, VM, VM],
        out_specs=(ANY, VM),
        scratch_shapes=plane_scratch(128)
        + [
            pltpu.VMEM((256, 128), F32),
            pltpu.VMEM((4, 2, 128, 256), F32),
            pltpu.VMEM((4, 2, 128, 256), F32),
            pltpu.VMEM((6, 128, 256), F32),
            pltpu.VMEM((256, 256), F32),
            pltpu.VMEM((256, 256), F32),
            pltpu.VMEM((256, 256), F32),
            pltpu.VMEM((2, 128, 256), F32),
            pltpu.VMEM((2, 384, 128), F32),
            pltpu.VMEM((384, 128), F32),
            pltpu.VMEM((4, 96, 128), F32),
            pltpu.VMEM((6, 96, 128), F32),
            pltpu.VMEM((4, 24, 128), F32),
            pltpu.VMEM((6, 24, 128), F32),
        ]
        + sems(100)
        + [pltpu.SemaphoreType.DMA],
        compiler_params=params(1),
        name="middle",
    )(fwd, adj, weight_in, weight_out)

    fwd2 = pl.pallas_call(
        second_product_kernel,
        out_shape=shape(33, 128, 256),
        in_specs=[SM, SM, ANY, VM],
        out_specs=VM,
        scratch_shapes=[
            pltpu.VMEM((slots, 128, 128), F32),
            pltpu.VMEM((16, 128, 256), BF16),
            pltpu.VMEM((16, 128, 256), BF16),
            pltpu.SemaphoreType.DMA((slots // CHUNK,)),
        ],
        compiler_params=params(),
        name="second_product",
    )(rows, cols, tiles, s2.reshape(16, 128, 256))

    return pl.pallas_call(
        last_kernel,
        out_shape=(shape(256, 256), shape(128, 256), shape(256, 256)),
        in_specs=[VM, VM],
        out_specs=(VM, VM, VM),
        scratch_shapes=plane_scratch(256)
        + [
            pltpu.VMEM((4, 24, 128), F32),
            pltpu.VMEM((4, 24, 128), F32),
            pltpu.VMEM((4, 96, 128), F32),
            pltpu.VMEM((4, 96, 128), F32),
        ]
        + sems(80),
        compiler_params=params(2),
        name="last",
    )(fwd2, g)


def solution(mesh):
    return jax.shard_map(
        per_device,
        mesh=mesh,
        in_specs=(
            P("col", "row"),
            P("row", "col", None),
            P("row", "col", None),
            P("row", "col", None, None, None),
            P(),
            P(),
            P(("col", "row"), None),
        ),
        out_specs=(P(("col", "row"), None), P(), P()),
        check_vma=False,
    )
```

```python
import heapq
import math

import jax
import jax.numpy as jnp
from jax import lax
from jax.experimental import pallas as pl
from jax.experimental.pallas import tpu as pltpu
from jax.sharding import PartitionSpec as P

MESH = pl.DeviceIdType.MESH
F32 = jnp.float32
BF16 = jnp.bfloat16
VMEM_LIMIT = 60 * 1024 * 1024
CHUNK = 8


def split(v):
    hi = v.astype(BF16)
    return hi, (v - hi.astype(F32)).astype(BF16)


def dot16(a, b, dims=(((1,), (0,)), ((), ()))):
    return lax.dot_general(a, b, dims, preferred_element_type=F32)


def dot3(a, b, dims=(((1,), (0,)), ((), ()))):
    ah, al = split(a)
    bh, bl = split(b)
    return dot16(ah, bl, dims) + dot16(al, bh, dims) + dot16(ah, bh, dims)


class Copy:
    def __init__(self, src, dst, axis, shift):
        self.src, self.dst, self.axis, self.shift = src, dst, axis, shift
        self.bytes = 4 * math.prod(src.shape)
        self.copy = self.arrival = None


RATE = {"x": 45e3, "y": 45e3, "z": 45e3, "core": 250e3}
DELAY = {"x": 1.6, "y": 1.6, "z": 1.6, "core": 1.0}
WINDOW = 2.5


class Net:
    def __init__(self, send_sems, recv_sems):
        self.send_sems, self.recv_sems = send_sems, recv_sems
        self.copies = []
        i, j = lax.axis_index("row"), lax.axis_index("col")
        self.x, self.core = i // 2, lax.rem(i, 2)
        self.z, self.y = j // 4, lax.rem(j, 4)
        self.i, self.j = i, j
        self.active, self.pending, self.free = [], {}, {}
        self.now, self.count = 0.0, 0

    def pos(self, axis):
        return {"x": self.x, "y": self.y, "z": self.z}[axis]

    def at(self, axis, shift):
        return lax.rem(self.pos(axis) + (shift + 4), 4)

    def peer(self, axis, shift):
        if axis == "core":
            return (self.x * 2 + 1 - self.core, self.j)
        p = self.at(axis, shift)
        if axis == "x":
            return (p * 2 + self.core, self.j)
        if axis == "y":
            return (self.i, self.z * 4 + p)
        return (self.i, p * 4 + self.y)

    def barrier(self, axes):
        sem = pltpu.get_barrier_semaphore()
        n = 0
        for axis in axes:
            for shift in (1,) if axis == "core" else (1, -1):
                pl.semaphore_signal(sem, inc=1, device_id=self.peer(axis, shift), device_id_type=MESH)
                n += 1
        pl.semaphore_wait(sem, n)

    def send(self, src, dst, axis, shift=1, level=5):
        copy = Copy(src, dst, axis, shift)
        self.count += 1
        heapq.heappush(self.pending.setdefault((axis, shift), []), (level, self.count, copy))
        return copy

    def pump(self):
        for link, heap in self.pending.items():
            while heap and self.free.get(link, 0.0) < self.now + WINDOW:
                one = heapq.heappop(heap)[2]
                k = len(self.copies)
                one.copy = pltpu.make_async_remote_copy(
                    src_ref=one.src,
                    dst_ref=one.dst,
                    send_sem=self.send_sems.at[k],
                    recv_sem=self.recv_sems.at[k],
                    device_id=self.peer(one.axis, one.shift),
                    device_id_type=MESH,
                )
                one.copy.start()
                self.copies.append(one.copy)
                end = max(self.now, self.free.get(link, 0.0)) + one.bytes / RATE[one.axis]
                self.free[link] = end
                one.arrival = end + DELAY[one.axis]

    def spawn(self, gen):
        self.active.append([gen, None])

    def run(self):
        while True:
            moved = True
            while moved:
                moved = False
                for entry in list(self.active):
                    if entry[1] is None or (callable(entry[1]) and entry[1]()):
                        moved = True
                        self.step(entry)
            self.pump()
            waits = [e for e in self.active if isinstance(e[1], Copy) and e[1].arrival is not None]
            if waits:
                entry = min(waits, key=lambda e: e[1].arrival)
                self.now = max(self.now, entry[1].arrival)
                entry[1].copy.wait_recv()
                self.step(entry)
            elif any(self.pending.values()):
                self.now = min(self.free.get(link, 0.0) for link, heap in self.pending.items() if heap)
            else:
                break
        assert not self.active
        for copy in self.copies:
            copy.wait_send()

    def step(self, entry):
        try:
            entry[1] = next(entry[0])
        except StopIteration:
            self.active.remove(entry)


def arrive(copy, have=None):
    yield copy
    if have is not None:
        have()


def ag_unit(net, axis, src, ref, have, way, level=5):
    p = net.at(axis, 0)
    near = net.send(src, ref(p), axis, way, level)
    other = net.send(src, ref(p), axis, -way, level)

    def chain():
        yield near
        pos = net.at(axis, -way)
        onward = net.send(ref(pos), ref(pos), axis, way, level)
        have(pos)
        yield onward
        have(net.at(axis, 2))

    net.spawn(chain())
    net.spawn(arrive(other, lambda: have(net.at(axis, way))))


def rs_unit(net, axis, part, ready, stage, emit, way, level=5, after=None):
    r, m, q = (stage(k) for k in range(3))
    box = []
    after = level if after is None else after

    def near():
        yield lambda: ready[-way]
        box.append(net.send(part(net.at(axis, -way)), q, axis, -way, level))

    def far():
        yield lambda: ready[2]
        first = net.send(part(net.at(axis, 2)), r, axis, way, level)
        yield first
        yield lambda: ready[way]
        r[...] = r[...] + part(net.at(axis, way))[...]
        yield net.send(r, m, axis, way, after)
        yield lambda: box
        yield box[0]
        yield lambda: ready[0]
        emit(part(net.at(axis, 0))[...] + (m[...] + q[...]))

    net.spawn(far())
    net.spawn(near())


ALL = {0: True, 1: True, 2: True, -1: True}
SHIFTS = (2, 1, -1, 0)
WAYS = (1, -1)


def rs_plane(net, tiles, stage_one, middle, stage_two, out, done):
    for part, (first, second) in enumerate((("z", "y"), ("y", "z"))):
        for u, way in enumerate(WAYS):
            ready = {d: False for d in SHIFTS}
            for k, d in enumerate((2, way, -way, 0)):
                pos2 = net.at(second, d)

                def term(pos1, pos2=pos2, part=part, u=u, first=first):
                    block = pos1 * 4 + pos2 if first == "z" else pos2 * 4 + pos1
                    return tiles.at[2 * block + part, pl.ds(u * 64, 64), :]

                def land(s, part=part, u=u, k=k):
                    return stage_one.at[part, k, u, s]

                def emit(value, part=part, u=u, pos2=pos2, d=d, ready=ready):
                    middle[part, pos2, u] = value
                    ready[d] = True

                rs_unit(net, first, term, ALL, land, emit, way, level=3 + k, after=2)

            def term2(pos, part=part, u=u):
                return middle.at[part, pos, u]

            def land2(s, part=part, u=u):
                return stage_two.at[part, u, s]

            def emit2(value, part=part, u=u):
                out[pl.ds(part * 128 + u * 64, 64), :] = value
                done.append((part, u))

            rs_unit(net, second, term2, ready, land2, emit2, way, level=1)


def gather_kernel(feat_ref, cot_ref, xt_ref, cots_ref, send_sems, recv_sems, local_sems):
    net = Net(send_sems, recv_sems)
    net.barrier(("x", "core", "y", "z"))
    own = [
        pltpu.make_async_copy(feat_ref, xt_ref.at[net.i], local_sems.at[0]),
        pltpu.make_async_copy(cot_ref, cots_ref.at[net.j], local_sems.at[1]),
    ]
    for copy in own:
        copy.start()

    def to_sibling(src, dst):
        net.spawn(arrive(net.send(src, dst, "core")))

    for u, way in enumerate(WAYS):
        half = pl.ds(u * 8, 8)

        def row_ref(pos, half=half):
            return xt_ref.at[pos * 2 + net.core, half, :]

        def row_have(pos, row_ref=row_ref):
            to_sibling(row_ref(pos), row_ref(pos))

        ag_unit(net, "x", feat_ref.at[half, :], row_ref, row_have, way)
    to_sibling(feat_ref, xt_ref.at[net.i])

    for part, (first, second) in enumerate((("y", "z"), ("z", "y"))):
        for u, way in enumerate(WAYS):
            rows = pl.ds(part * 128 + u * 64, 64)

            def ref(pos1, pos2, rows=rows, first=first):
                block = pos1 + pos2 * 4 if first == "y" else pos1 * 4 + pos2
                return cots_ref.at[block, rows, :]

            def start_second(pos1, src=None, ref=ref, second=second, way=way):
                src = ref(pos1, net.at(second, 0)) if src is None else src
                ag_unit(net, second, src, lambda pos2: ref(pos1, pos2), lambda pos: None, way)

            ag_unit(net, first, cot_ref.at[rows, :], lambda pos1, ref=ref, second=second: ref(pos1, net.at(second, 0)),
                    start_second, way, level=1)
            start_second(net.at(first, 0), cot_ref.at[rows, :])
    net.run()
    for copy in own:
        copy.wait()


def tile_copies(tiles_ref, buf, sems):
    n = tiles_ref.shape[0] // CHUNK
    return [
        pltpu.make_async_copy(tiles_ref.at[pl.ds(k * CHUNK, CHUNK)], buf.at[pl.ds(k * CHUNK, CHUNK)], sems.at[k])
        for k in range(n)
    ]


def wait_chunk(tiles_ref, buf, sems, k):
    rows = pl.ds(k * CHUNK, CHUNK)
    pltpu.make_async_copy(tiles_ref.at[rows], buf.at[rows], sems.at[k]).wait()


def first_products_kernel(rows_ref, cols_ref, tiles_ref, xt_ref, cots_ref, fwd_ref, adj_ref,
                          buf, cbuf, xh, xl, ch, cl, sems, csem):
    copies = tile_copies(tiles_ref, buf, sems)
    for copy in copies:
        copy.start()
    ccopy = pltpu.make_async_copy(cots_ref, cbuf, csem)
    ccopy.start()
    fwd_ref[...] = jnp.zeros_like(fwd_ref)
    adj_ref[...] = jnp.zeros_like(adj_ref)

    def split_x(c, _):
        h, l = split(jnp.transpose(xt_ref[:, pl.ds(pl.multiple_of(c * 128, 128), 128)]))
        xh[c] = h
        xl[c] = l
        return 0

    lax.fori_loop(0, 16, split_x, 0)

    def fwd(k, _):
        wait_chunk(tiles_ref, buf, sems, k)
        for s in range(CHUNK):
            t = k * CHUNK + s
            r, c = rows_ref[t], cols_ref[t]
            h, l = split(buf[t])
            w = jnp.concatenate([xh[c], xl[c]], axis=1)
            res = dot16(jnp.concatenate([h, l], axis=1), jnp.concatenate([w, w], axis=0))
            fwd_ref[r] += res[:, :128] + res[:, 128:]
        return 0

    lax.fori_loop(0, len(copies), fwd, 0)
    ccopy.wait()

    def split_c(r, _):
        h, l = split(cbuf[r])
        ch[r] = h
        cl[r] = l
        return 0

    lax.fori_loop(0, 32, split_c, 0)

    def adj(k, _):
        for s in range(CHUNK):
            t = k * CHUNK + s
            r, c = rows_ref[t], cols_ref[t]
            target = jnp.where(r < 32, c, 16)
            r = jnp.minimum(r, 31)
            h, l = split(jnp.transpose(buf[t]))
            w = ch[r]
            res = dot16(jnp.concatenate([h, l], axis=1), jnp.concatenate([w, w], axis=0))
            adj_ref[target] += res + dot16(h, cl[r])
        return 0

    lax.fori_loop(0, len(copies), adj, 0)


def second_product_kernel(rows_ref, cols_ref, tiles_ref, s_ref, fwd_ref, buf, xh, xl, sems):
    copies = tile_copies(tiles_ref, buf, sems)
    for copy in copies:
        copy.start()
    fwd_ref[...] = jnp.zeros_like(fwd_ref)

    def split_x(c, _):
        h, l = split(s_ref[c])
        xh[c] = h
        xl[c] = l
        return 0

    lax.fori_loop(0, 16, split_x, 0)

    def fwd(k, _):
        wait_chunk(tiles_ref, buf, sems, k)
        for s in range(CHUNK):
            t = k * CHUNK + s
            r, c = rows_ref[t], cols_ref[t]
            h, l = split(buf[t])
            w = xh[c]
            res = dot16(jnp.concatenate([h, l], axis=1), jnp.concatenate([w, w], axis=0))
            fwd_ref[r] += res + dot16(h, xl[c])
        return 0

    lax.fori_loop(0, len(copies), fwd, 0)


def middle_kernel(fwd_ref, adj_ref, win_ref, wout_ref, s2_ref, g_ref,
                  stage_a, mid_a, stage_b, s_buf, stage_c, mid_c, stage_d, d_buf, h_buf, p_buf, s2_buf,
                  g_buf, stage_e, g_one, stage_f, g_two, stage_g, send_sems, recv_sems, local_sem):
    net = Net(send_sems, recv_sems)
    net.barrier(("x", "core", "y", "z"))
    done_s, done_d = [], []
    rs_plane(net, fwd_ref, stage_a, mid_a, stage_b, s_buf, done_s)

    for u, way in enumerate(WAYS):
        ready = {d: False for d in SHIFTS}
        for k, d in enumerate((2, way, -way, 0)):
            pos = net.at("x", d)

            def cores(u=u, k=k, d=d, pos=pos, ready=ready):
                block = pos * 2 + 1 - net.core
                land = stage_c.at[u, k]
                yield net.send(adj_ref.at[block * 2 + u], land, "core", 1, k)
                mid_c[u, pos] = adj_ref[(pos * 2 + net.core) * 2 + u] + land[...]
                ready[d] = True

            net.spawn(cores())

        def emit_d(value, u=u):
            d_buf[pl.ds(u * 128, 128), :] = value
            done_d.append(u)

        rs_unit(net, "x", lambda pos, u=u: mid_c.at[u, pos], ready, lambda s, u=u: stage_d.at[u, s], emit_d, way)
    local = pltpu.make_async_copy(s2_buf, s2_ref.at[net.i], local_sem)

    def dense():
        yield lambda: len(done_s) == 4
        pre = dot3(s_buf[...], win_ref[...])
        hidden = pre * (1.0 / (1.0 + jnp.exp(-pre)))
        p_buf[...] = pre
        h_buf[...] = hidden
        s2_buf[...] = dot3(hidden, wout_ref[...]).reshape(2, 128, 256)
        local.start()
        net.now += 1.5
        for u, way in enumerate(WAYS):

            def ref(pos, u=u):
                return s2_ref.at[pos * 2 + net.core, u]

            def have(pos, ref=ref):
                net.spawn(arrive(net.send(ref(pos), ref(pos), "core")))

            ag_unit(net, "x", s2_buf.at[u], ref, have, way)
        net.spawn(arrive(net.send(s2_buf, s2_ref.at[net.i], "core")))
        net.spawn(grads())

    def grads():
        yield lambda: len(done_d) == 2
        net.pump()
        d = d_buf[...]
        pre = p_buf[...]
        sg = 1.0 / (1.0 + jnp.exp(-pre))
        d_pre = dot3(d, wout_ref[...], (((1,), (1,)), ((), ()))) * sg * (1.0 + pre * (1.0 - sg))
        grad_in = dot3(jnp.transpose(s_buf[...]), d_pre)
        grad_out = dot3(jnp.transpose(h_buf[...]), d)
        for c in range(2):
            lanes = slice(c * 128, c * 128 + 128)
            g_buf[c, pl.ds(0, 128), :] = grad_in[:, lanes]
            g_buf[c, pl.ds(128, 256), :] = grad_out[:, lanes]
        net.now += 2.0
        yield net.send(g_buf.at[1 - net.core], stage_e, "core", 1, 0)
        g_one[...] = (g_buf[net.core] + stage_e[...]).reshape(g_one.shape)
        one = []

        def emit_one(value):
            g_two[...] = value.reshape(g_two.shape)
            one.append(0)

        rs_unit(net, "y", lambda pos: g_one.at[pos], ALL, lambda s: stage_f.at[s], emit_one, 1)
        yield lambda: one

        def emit_two(value):
            g_ref[...] = value

        rs_unit(net, "z", lambda pos: g_two.at[pos], ALL, lambda s: stage_g.at[s], emit_two, 1)

    net.spawn(dense())
    net.run()
    local.wait()


def last_kernel(fwd_ref, g_ref, out_ref, gin_ref, gout_ref,
                stage_a, mid_a, stage_b, gx, gz, gy, gsib, send_sems, recv_sems):
    net = Net(send_sems, recv_sems)
    net.barrier(("x", "core", "y", "z"))

    def grads():
        def walk(axis, src, dst):
            got = []
            ag_unit(net, axis, src, lambda pos: dst.at[pos], got.append, 1, 0)
            yield lambda: len(got) == 3

        gx[net.x] = g_ref[...]
        yield from walk("x", g_ref, gx)
        gz[net.z] = (gx[0] + gx[1]) + (gx[2] + gx[3])
        yield from walk("z", gz.at[net.z], gz)
        gy[net.y] = gz[...].reshape(96, 128)
        yield from walk("y", gy.at[net.y], gy)
        yield net.send(gy, gsib, "core", 1, 0)
        mine, other = gy[...].reshape(384, 128), gsib[...].reshape(384, 128)
        first = net.core == 0
        low = jnp.where(first, mine, other)
        high = jnp.where(first, other, mine)
        gin_ref[:, :128] = low[:128]
        gin_ref[:, 128:] = high[:128]
        gout_ref[:, :128] = low[128:]
        gout_ref[:, 128:] = high[128:]

    net.spawn(grads())
    rs_plane(net, fwd_ref, stage_a, mid_a, stage_b, out_ref, [])
    net.run()


ANY = pl.BlockSpec(memory_space=pl.ANY)
VM = pl.BlockSpec(memory_space=pltpu.VMEM)
SM = pl.BlockSpec(memory_space=pltpu.SMEM)


def params(collective_id=None):
    return pltpu.CompilerParams(
        collective_id=collective_id,
        has_side_effects=collective_id is not None,
        vmem_limit_bytes=VMEM_LIMIT,
    )


def sems(n):
    return [pltpu.SemaphoreType.DMA((n,)), pltpu.SemaphoreType.DMA((n,))]


def plane_scratch(width):
    return [
        pltpu.VMEM((2, 4, 2, 3, 64, width), F32),
        pltpu.VMEM((2, 4, 2, 64, width), F32),
        pltpu.VMEM((2, 2, 3, 64, width), F32),
    ]


def shape(*dims):
    return jax.ShapeDtypeStruct(dims, F32)


def per_device(features, tile_rows, tile_cols, tile_values, weight_in, weight_out, cotangent):
    slots = tile_rows.shape[-1]
    rows, cols = tile_rows.reshape(slots), tile_cols.reshape(slots)
    tiles = tile_values.reshape(slots, 128, 128)

    xt, cots = pl.pallas_call(
        gather_kernel,
        out_shape=(shape(8, 16, 2048), shape(16, 256, 256)),
        in_specs=[ANY, ANY],
        out_specs=(ANY, ANY),
        scratch_shapes=sems(100) + [pltpu.SemaphoreType.DMA((2,))],
        compiler_params=params(0),
        name="gather",
    )(features.T, cotangent)

    fwd, adj = pl.pallas_call(
        first_products_kernel,
        out_shape=(shape(33, 128, 128), shape(17, 128, 256)),
        in_specs=[SM, SM, ANY, VM, ANY],
        out_specs=(VM, VM),
        scratch_shapes=[
            pltpu.VMEM((slots, 128, 128), F32),
            pltpu.VMEM((32, 128, 256), F32),
            pltpu.VMEM((16, 128, 128), BF16),
            pltpu.VMEM((16, 128, 128), BF16),
            pltpu.VMEM((32, 128, 256), BF16),
            pltpu.VMEM((32, 128, 256), BF16),
            pltpu.SemaphoreType.DMA((slots // CHUNK,)),
            pltpu.SemaphoreType.DMA,
        ],
        compiler_params=params(),
        name="first_products",
    )(rows, cols, tiles, xt.reshape(128, 2048), cots.reshape(32, 128, 256))

    s2, g = pl.pallas_call(
        middle_kernel,
        out_shape=(shape(8, 2, 128, 256), shape(24, 128)),
        in_specs=[VM, VM, VM, VM],
        out_specs=(ANY, VM),
        scratch_shapes=plane_scratch(128)
        + [
            pltpu.VMEM((256, 128), F32),
            pltpu.VMEM((2, 4, 128, 256), F32),
            pltpu.VMEM((2, 4, 128, 256), F32),
            pltpu.VMEM((2, 3, 128, 256), F32),
            pltpu.VMEM((256, 256), F32),
            pltpu.VMEM((256, 256), F32),
            pltpu.VMEM((256, 256), F32),
            pltpu.VMEM((2, 128, 256), F32),
            pltpu.VMEM((2, 384, 128), F32),
            pltpu.VMEM((384, 128), F32),
            pltpu.VMEM((4, 96, 128), F32),
            pltpu.VMEM((3, 96, 128), F32),
            pltpu.VMEM((4, 24, 128), F32),
            pltpu.VMEM((3, 24, 128), F32),
        ]
        + sems(120)
        + [pltpu.SemaphoreType.DMA],
        compiler_params=params(1),
        name="middle",
    )(fwd, adj, weight_in, weight_out)

    fwd2 = pl.pallas_call(
        second_product_kernel,
        out_shape=shape(33, 128, 256),
        in_specs=[SM, SM, ANY, VM],
        out_specs=VM,
        scratch_shapes=[
            pltpu.VMEM((slots, 128, 128), F32),
            pltpu.VMEM((16, 128, 256), BF16),
            pltpu.VMEM((16, 128, 256), BF16),
            pltpu.SemaphoreType.DMA((slots // CHUNK,)),
        ],
        compiler_params=params(),
        name="second_product",
    )(rows, cols, tiles, s2.reshape(16, 128, 256))

    return pl.pallas_call(
        last_kernel,
        out_shape=(shape(256, 256), shape(128, 256), shape(256, 256)),
        in_specs=[VM, VM],
        out_specs=(VM, VM, VM),
        scratch_shapes=plane_scratch(256)
        + [
            pltpu.VMEM((4, 24, 128), F32),
            pltpu.VMEM((4, 24, 128), F32),
            pltpu.VMEM((4, 96, 128), F32),
            pltpu.VMEM((4, 96, 128), F32),
        ]
        + sems(100),
        compiler_params=params(2),
        name="last",
    )(fwd2, g)


def solution(mesh):
    return jax.shard_map(
        per_device,
        mesh=mesh,
        in_specs=(
            P("col", "row"),
            P("row", "col", None),
            P("row", "col", None),
            P("row", "col", None, None, None),
            P(),
            P(),
            P(("col", "row"), None),
        ),
        out_specs=(P(("col", "row"), None), P(), P()),
        check_vma=False,
    )
```

```python
import heapq
import math
import types

import jax
import jax.numpy as jnp
from jax import lax
from jax.experimental import pallas as pl
from jax.experimental.pallas import tpu as pltpu
from jax.sharding import PartitionSpec as P

MESH = pl.DeviceIdType.MESH
F32 = jnp.float32
BF16 = jnp.bfloat16
VMEM_LIMIT = 67043328
CHUNK = 8
SLOTS = 80
TROWS = 32
TCOLS = 16
COPIES = 240


def split(v):
    hi = v.astype(BF16)
    return hi, (v - hi.astype(F32)).astype(BF16)


def dot16(a, b, dims=(((1,), (0,)), ((), ()))):
    return lax.dot_general(a, b, dims, preferred_element_type=F32)


def dot3(a, b, dims=(((1,), (0,)), ((), ()))):
    ah, al = split(a)
    bh, bl = split(b)
    return dot16(ah, bl, dims) + dot16(al, bh, dims) + dot16(ah, bh, dims)


class Copy:
    def __init__(self, src, dst, axis, shift):
        self.src, self.dst, self.axis, self.shift = src, dst, axis, shift
        self.bytes = 4 * math.prod(src.shape)
        self.copy = self.arrival = None


RATE = {"x": 45e3, "y": 45e3, "z": 45e3, "core": 250e3}
DELAY = {"x": 1.6, "y": 1.6, "z": 1.6, "core": 1.0}
WINDOW = 2.5


class Tick:
    def __init__(self, net, spent, level):
        net.now += spent
        self.arrival = net.now + level * 1e-3


class Net:
    def __init__(self, send_sems, recv_sems):
        self.send_sems, self.recv_sems = send_sems, recv_sems
        self.copies = []
        i, j = lax.axis_index("row"), lax.axis_index("col")
        self.x, self.core = i // 2, lax.rem(i, 2)
        self.z, self.y = j // 4, lax.rem(j, 4)
        self.i, self.j = i, j
        self.active, self.pending, self.free = [], {}, {}
        self.now, self.count = 0.0, 0

    def pos(self, axis):
        return {"x": self.x, "y": self.y, "z": self.z}[axis]

    def at(self, axis, shift):
        return lax.rem(self.pos(axis) + (shift + 4), 4)

    def peer(self, axis, shift):
        if axis == "core":
            return (self.x * 2 + 1 - self.core, self.j)
        p = self.at(axis, shift)
        if axis == "x":
            return (p * 2 + self.core, self.j)
        if axis == "y":
            return (self.i, self.z * 4 + p)
        return (self.i, p * 4 + self.y)

    def barrier(self, axes):
        sem = pltpu.get_barrier_semaphore()
        n = 0
        for axis in axes:
            for shift in (1,) if axis == "core" else (1, -1):
                pl.semaphore_signal(sem, inc=1, device_id=self.peer(axis, shift), device_id_type=MESH)
                n += 1
        pl.semaphore_wait(sem, n)

    def send(self, src, dst, axis, shift=1, level=5):
        copy = Copy(src, dst, axis, shift)
        self.count += 1
        heapq.heappush(self.pending.setdefault((axis, shift), []), (level, self.count, copy))
        return copy

    def pump(self):
        for link, heap in self.pending.items():
            while heap and self.free.get(link, 0.0) < self.now + WINDOW:
                one = heapq.heappop(heap)[2]
                k = len(self.copies)
                one.copy = pltpu.make_async_remote_copy(
                    src_ref=one.src,
                    dst_ref=one.dst,
                    send_sem=self.send_sems.at[k],
                    recv_sem=self.recv_sems.at[k],
                    device_id=self.peer(one.axis, one.shift),
                    device_id_type=MESH,
                )
                one.copy.start()
                self.copies.append(one.copy)
                end = max(self.now, self.free.get(link, 0.0)) + one.bytes / RATE[one.axis]
                self.free[link] = end
                one.arrival = end + DELAY[one.axis]

    def spawn(self, gen):
        self.active.append([gen, None])

    def run(self):
        while True:
            moved = True
            while moved:
                moved = False
                for entry in list(self.active):
                    if entry[1] is None or (callable(entry[1]) and entry[1]()):
                        moved = True
                        self.step(entry)
            self.pump()
            waits = [e for e in self.active if not callable(e[1]) and e[1].arrival is not None]
            if waits:
                entry = min(waits, key=lambda e: e[1].arrival)
                self.now = max(self.now, entry[1].arrival)
                if isinstance(entry[1], Copy):
                    entry[1].copy.wait_recv()
                self.step(entry)
            elif any(self.pending.values()):
                self.now = min(self.free.get(link, 0.0) for link, heap in self.pending.items() if heap)
            else:
                break
        assert not self.active
        for copy in self.copies:
            copy.wait_send()

    def step(self, entry):
        try:
            entry[1] = next(entry[0])
        except StopIteration:
            self.active.remove(entry)


def arrive(copy, have=None):
    yield copy
    if have is not None:
        have()


def ag_unit(net, axis, src, ref, have, way, level=5):
    p = net.at(axis, 0)
    near = net.send(src, ref(p), axis, way, level)
    other = net.send(src, ref(p), axis, -way, level)

    def chain():
        yield near
        pos = net.at(axis, -way)
        onward = net.send(ref(pos), ref(pos), axis, way, level)
        have(pos)
        yield onward
        have(net.at(axis, 2))

    net.spawn(chain())
    net.spawn(arrive(other, lambda: have(net.at(axis, way))))


def rs_unit(net, axis, part, ready, stage, emit, way, level=5, after=None):
    r, m, q = (stage(k) for k in range(3))
    box = []
    after = level if after is None else after

    def near():
        yield lambda: ready[-way]
        box.append(net.send(part(net.at(axis, -way)), q, axis, -way, level))

    def far():
        yield lambda: ready[2]
        first = net.send(part(net.at(axis, 2)), r, axis, way, level)
        yield first
        yield lambda: ready[way]
        r[...] = r[...] + part(net.at(axis, way))[...]
        yield net.send(r, m, axis, way, after)
        yield lambda: box
        yield box[0]
        yield lambda: ready[0]
        emit(part(net.at(axis, 0))[...] + (m[...] + q[...]))

    net.spawn(far())
    net.spawn(near())


ALL = {0: True, 1: True, 2: True, -1: True}
SHIFTS = (2, 1, -1, 0)
WAYS = (1, -1)


def rs_plane(net, tiles, stage_one, middle, stage_two, out, done):
    for part, (first, second) in enumerate((("z", "y"), ("y", "z"))):
        for u, way in enumerate(WAYS):
            ready = {d: False for d in SHIFTS}
            for k, d in enumerate((2, way, -way, 0)):
                pos2 = net.at(second, d)

                def term(pos1, pos2=pos2, part=part, u=u, first=first):
                    block = pos1 * 4 + pos2 if first == "z" else pos2 * 4 + pos1
                    return tiles.at[2 * block + part, pl.ds(u * 64, 64), :]

                def land(s, part=part, u=u, k=k):
                    return stage_one.at[part, k, u, s]

                def emit(value, part=part, u=u, pos2=pos2, d=d, ready=ready):
                    middle[part, pos2, u] = value
                    ready[d] = True

                rs_unit(net, first, term, ALL, land, emit, way, level=3 + k, after=2)

            def term2(pos, part=part, u=u):
                return middle.at[part, pos, u]

            def land2(s, part=part, u=u):
                return stage_two.at[part, u, s]

            def emit2(value, part=part, u=u):
                out[pl.ds(part * 128 + u * 64, 64), :] = value
                done.append((part, u))

            rs_unit(net, second, term2, ready, land2, emit2, way, level=1)


def tables_kernel(rows_ref, cols_ref, int_ref, float_ref, pad):
    pad[0:1, :] = jnp.full((1, 128), TROWS, jnp.int32)
    pad[1:2, :] = jnp.zeros((1, 128), jnp.int32)
    pad[0:1, :SLOTS] = rows_ref[...]
    pad[1:2, :SLOTS] = cols_ref[...]
    lane = lax.broadcasted_iota(jnp.int32, (128, 128), 1)
    line = lax.broadcasted_iota(jnp.int32, (128, 128), 0)

    def wide(v):
        return jnp.broadcast_to(v, (128, 128))

    def count(v):
        return jnp.sum(v, axis=0, keepdims=True)

    row, col = pad[0:1, :], pad[1:2, :]
    used = row < TROWS
    for major, minor, size, k in ((row, col, TROWS, 0), (col, row, TCOLS, 3)):
        major, minor = jnp.where(used, major, size), jnp.where(used, minor, 0)
        key = wide(major * 64 + minor)
        key_t = jnp.transpose(key)
        before = (key_t < key) | ((key_t == key) & (line < lane))
        rank_t = jnp.transpose(wide(count(before.astype(jnp.int32))))
        here = rank_t == lane
        order = count(jnp.where(here, line, 0))
        sorted_key = count(jnp.where(here, key_t, 0))
        group = sorted_key // 64
        group_t = jnp.transpose(wide(group))
        found = count((group_t == lane).astype(jnp.int32)) > 0
        last = jnp.where(found, count((group_t <= lane).astype(jnp.int32)), 0)
        int_ref[k : k + 1, :] = order
        int_ref[k + 1 : k + 2, :] = sorted_key - group * 64
        int_ref[k + 2 : k + 3, :] = last
        same = count(((group_t == wide(group)) & (line + 1 == lane)).astype(jnp.int32))
        float_ref[k : k + 1, :] = same.astype(F32)


SCRATCH = {
    "buf": ((2, CHUNK, 128, 128), F32),
    "acat": ((SLOTS, 128, 256), BF16),
    "atc": ((SLOTS, 128, 256), BF16),
    "sums_f": ((SLOTS + 1, 128, 256), F32),
    "sums_a": ((SLOTS + 1, 128, 256), F32),
    "xt": ((8, 16, 2048), F32),
    "xh": ((16, 128, 128), BF16),
    "xl": ((16, 128, 128), BF16),
    "cots": ((32, 128, 256), F32),
    "s2": ((16, 128, 256), F32),
    "fwd1": ((32, 128, 128), F32),
    "fwd2": ((32, 128, 256), F32),
    "adj": ((16, 128, 256), F32),
    "a1": ((2, 4, 2, 3, 64, 128), F32),
    "m1": ((2, 4, 2, 64, 128), F32),
    "b1": ((2, 2, 3, 64, 128), F32),
    "a2": ((2, 4, 2, 3, 64, 256), F32),
    "m2": ((2, 4, 2, 64, 256), F32),
    "b2": ((2, 2, 3, 64, 256), F32),
    "c3": ((2, 4, 128, 256), F32),
    "m3": ((2, 4, 128, 256), F32),
    "d3": ((2, 3, 128, 256), F32),
    "s": ((256, 128), F32),
    "d": ((256, 256), F32),
    "h": ((256, 256), F32),
    "p": ((256, 256), F32),
    "g": ((2, 384, 128), F32),
    "ge": ((384, 128), F32),
    "g1": ((4, 96, 128), F32),
    "gf": ((3, 96, 128), F32),
    "g2": ((4, 24, 128), F32),
    "gg": ((3, 24, 128), F32),
    "gs": ((24, 128), F32),
    "gx": ((4, 24, 128), F32),
    "gz": ((4, 24, 128), F32),
    "gy": ((4, 96, 128), F32),
    "gsib": ((4, 96, 128), F32),
}
BLOCK = 16
UNROLL = 4


def step_kernel(int_ref, float_ref, feat_ref, cot_ref, tiles_ref, win_ref, wout_ref,
                out_ref, gin_ref, gout_ref, *scratch):
    w = types.SimpleNamespace(**dict(zip(SCRATCH, scratch)))
    send_sems, recv_sems, local_sems = scratch[len(SCRATCH):]
    chunks = SLOTS // CHUNK

    def chunk_copy(k):
        return pltpu.make_async_copy(tiles_ref.at[pl.ds(k * CHUNK, CHUNK)], w.buf.at[k % 2], local_sems.at[k])

    net = Net(send_sems, recv_sems)
    loads = [chunk_copy(k) for k in range(chunks)]
    loads[0].start()
    loads[1].start()
    own_x = pltpu.make_async_copy(feat_ref, w.xt.at[net.i], local_sems.at[chunks])
    own_c = pltpu.make_async_copy(
        cot_ref, w.cots.at[pl.ds(net.j * 2, 2)], local_sems.at[chunks + 1])
    own_x.start()
    own_c.start()
    w.sums_f[0] = jnp.zeros_like(w.sums_f[0])
    w.sums_a[0] = jnp.zeros_like(w.sums_a[0])
    net.barrier(("x", "core", "y", "z"))
    seen = {"x": 0, "cot": 0, "s2": 0}
    done = {}

    def saw(name):
        seen[name] += 1

    def row_gather(name, src, ref_of, own_src, own_dst):
        for u, way in enumerate(WAYS):

            def ref(pos, u=u):
                return ref_of(pos * 2 + net.core, u)

            def have(pos, ref=ref):
                saw(name)
                net.spawn(arrive(net.send(ref(pos), ref(pos), "core"), lambda: saw(name)))

            ag_unit(net, "x", src(u), ref, have, way, 0)
        net.spawn(arrive(net.send(own_src, own_dst, "core"), lambda: saw(name)))

    def halves(u):
        return pl.ds(u * 8, 8)

    row_gather("x", lambda u: feat_ref.at[halves(u), :], lambda i, u: w.xt.at[i, halves(u), :],
               feat_ref, w.xt.at[net.i])

    for part, (first, second) in enumerate((("y", "z"), ("z", "y"))):
        for u, way in enumerate(WAYS):
            rows = pl.ds(u * 64, 64)
            src = cot_ref.at[part, rows, :]

            def ref(pos1, pos2, rows=rows, first=first, part=part):
                block = pos1 + pos2 * 4 if first == "y" else pos1 * 4 + pos2
                return w.cots.at[2 * block + part, rows, :]

            def start_second(pos1, src=None, ref=ref, second=second, way=way):
                src = ref(pos1, net.at(second, 0)) if src is None else src
                ag_unit(net, second, src, lambda pos2: ref(pos1, pos2), lambda pos: saw("cot"), way, 12)

            def have_one(pos1, start_second=start_second):
                saw("cot")
                start_second(pos1)

            ag_unit(net, first, src, lambda pos1, ref=ref, second=second: ref(pos1, net.at(second, 0)),
                    have_one, way, level=11)
            start_second(net.at(first, 0), src)

    def sums(base, k, lhs, product, store):
        def body(q, _):
            acc = None
            for v in range(UNROLL):
                n = base + q * UNROLL + v
                prev = store(n)[...] if acc is None else acc
                acc = prev * float_ref[k, n] + product(lhs[int_ref[k, n]], int_ref[k + 1, n])
                store(n + 1)[...] = acc
            return 0

        lax.fori_loop(0, BLOCK // UNROLL, body, 0)

    def pick(k, count, load, out):
        def body(r, _):
            out[r] = load(int_ref[k + 2, r])
            return 0

        lax.fori_loop(0, count, body, 0)

    def wide_product(values):
        def product(left, n):
            h, l = split(values[n])
            return dot16(left, jnp.concatenate([h, h], axis=0)) + dot16(left[:, :128], l)

        return product

    def narrow_product(left, n):
        pair = jnp.concatenate([w.xh[n], w.xl[n]], axis=1)
        res = dot16(left, jnp.concatenate([pair, pair], axis=0))
        return res[:, :128] + res[:, 128:]

    def tiles():
        for k in range(chunks):
            loads[k].wait()

            def body(n, _, k=k):
                h, l = split(w.buf[k % 2, n])
                w.acat[k * CHUNK + n] = jnp.concatenate([h, l], axis=1)
                return 0

            lax.fori_loop(0, CHUNK, body, 0)
            if k + 2 < chunks:
                loads[k + 2].start()
            yield Tick(net, 0.5, 0)
        done["acat"] = True
        for k in range(chunks):

            def turn(n, _, k=k):
                t = k * CHUNK + n
                both = w.acat[t]
                w.atc[t] = jnp.concatenate([jnp.transpose(both[:, :128]), jnp.transpose(both[:, 128:])], axis=1)
                return 0

            lax.fori_loop(0, CHUNK, turn, 0)
            yield Tick(net, 0.6, 5)
        done["atc"] = True

    def first_layer():
        yield lambda: seen["x"] == 13 and done.get("acat")
        own_x.wait()

        def split_x(c, _):
            piece = w.xt[:, :, pl.ds(pl.multiple_of(c * 128, 128), 128)].reshape(128, 128)
            h, l = split(jnp.transpose(piece))
            w.xh[c] = h
            w.xl[c] = l
            return 0

        lax.fori_loop(0, 16, split_x, 0)
        yield Tick(net, 1.0, 0)
        for base in range(0, SLOTS, BLOCK):
            sums(base, 0, w.acat, narrow_product, lambda n: w.sums_f.at[n, :, pl.ds(0, 128)])
            yield Tick(net, 1.2, 0)
        pick(0, 32, lambda n: w.sums_f[n, :, :128], w.fwd1)
        net.now += 0.5
        parts = []
        rs_plane(net, w.fwd1, w.a1, w.m1, w.b1, w.s, parts)
        yield lambda: len(parts) == 4
        pre = dot3(w.s[...], win_ref[...])
        hidden = pre * (1.0 / (1.0 + jnp.exp(-pre)))
        w.p[...] = pre
        w.h[...] = hidden
        mine = w.s2.at[pl.ds(net.i * 2, 2)]
        mine[...] = dot3(hidden, wout_ref[...]).reshape(2, 128, 256)
        net.now += 1.5
        row_gather("s2", lambda u: w.s2.at[net.i * 2 + u], lambda i, u: w.s2.at[i * 2 + u], mine, mine)
        done["pre"] = True
        yield lambda: seen["s2"] == 13
        for base in range(0, SLOTS, BLOCK):
            sums(base, 0, w.acat, wide_product(w.s2), lambda n: w.sums_f.at[n])
            yield Tick(net, 1.8, 1)
        pick(0, 32, lambda n: w.sums_f[n], w.fwd2)
        net.now += 0.8
        rs_plane(net, w.fwd2, w.a2, w.m2, w.b2, out_ref, [])

    def adjoint():
        yield lambda: seen["cot"] == 60 and done.get("atc")
        own_c.wait()
        for base in range(0, SLOTS, BLOCK):
            sums(base, 3, w.atc, wide_product(w.cots), lambda n: w.sums_a.at[n])
            yield Tick(net, 1.8, 2)
        pick(3, 16, lambda n: w.sums_a[n], w.adj)
        net.now += 0.5
        parts = []
        for u, way in enumerate(WAYS):
            ready = {d: False for d in SHIFTS}
            for k, d in enumerate((2, way, -way, 0)):
                pos = net.at("x", d)

                def cores(u=u, k=k, d=d, pos=pos, ready=ready):
                    land = w.c3.at[u, k]
                    yield net.send(w.adj.at[(pos * 2 + 1 - net.core) * 2 + u], land, "core", 1, k)
                    w.m3[u, pos] = w.adj[(pos * 2 + net.core) * 2 + u] + land[...]
                    ready[d] = True

                net.spawn(cores())

            def emit_d(value, u=u):
                w.d[pl.ds(u * 128, 128), :] = value
                parts.append(u)

            rs_unit(net, "x", lambda pos, u=u: w.m3.at[u, pos], ready, lambda k, u=u: w.d3.at[u, k], emit_d, way)
        yield lambda: len(parts) == 2 and done.get("pre")
        net.pump()
        d = w.d[...]
        pre = w.p[...]
        sg = 1.0 / (1.0 + jnp.exp(-pre))
        d_pre = dot3(d, wout_ref[...], (((1,), (1,)), ((), ()))) * sg * (1.0 + pre * (1.0 - sg))
        grad_in = dot3(jnp.transpose(w.s[...]), d_pre)
        grad_out = dot3(jnp.transpose(w.h[...]), d)
        for c in range(2):
            lanes = slice(c * 128, c * 128 + 128)
            w.g[c, pl.ds(0, 128), :] = grad_in[:, lanes]
            w.g[c, pl.ds(128, 256), :] = grad_out[:, lanes]
        net.now += 2.0
        yield net.send(w.g.at[1 - net.core], w.ge, "core", 1, 0)
        w.g1[...] = (w.g[net.core] + w.ge[...]).reshape(w.g1.shape)
        one, two = [], []

        def emit_one(value):
            w.g2[...] = value.reshape(w.g2.shape)
            one.append(0)

        rs_unit(net, "y", lambda pos: w.g1.at[pos], ALL, lambda k: w.gf.at[k], emit_one, 1, 0)
        yield lambda: one

        def emit_two(value):
            w.gs[...] = value
            two.append(0)

        rs_unit(net, "z", lambda pos: w.g2.at[pos], ALL, lambda k: w.gg.at[k], emit_two, 1, 0)
        yield lambda: two

        def walk(axis, src, dst):
            got = []
            ag_unit(net, axis, src, lambda pos: dst.at[pos], got.append, 1, 0)
            yield lambda: len(got) == 3

        w.gx[net.x] = w.gs[...]
        yield from walk("x", w.gs, w.gx)
        w.gz[net.z] = (w.gx[0] + w.gx[1]) + (w.gx[2] + w.gx[3])
        yield from walk("z", w.gz.at[net.z], w.gz)
        w.gy[net.y] = w.gz[...].reshape(96, 128)
        yield from walk("y", w.gy.at[net.y], w.gy)
        yield net.send(w.gy, w.gsib, "core", 1, 0)
        mine, other = w.gy[...].reshape(384, 128), w.gsib[...].reshape(384, 128)
        first = net.core == 0
        low = jnp.where(first, mine, other)
        high = jnp.where(first, other, mine)
        gin_ref[:, :128] = low[:128]
        gin_ref[:, 128:] = high[:128]
        gout_ref[:, :128] = low[128:]
        gout_ref[:, 128:] = high[128:]

    net.spawn(tiles())
    net.spawn(first_layer())
    net.spawn(adjoint())
    net.run()


def finish_kernel(a_ref, b_ref, c_ref, out_a, out_b, out_c):
    out_a[...] = a_ref[...]
    out_b[...] = b_ref[...]
    out_c[...] = c_ref[...]


ANY = pl.BlockSpec(memory_space=pl.ANY)
VM = pl.BlockSpec(memory_space=pltpu.VMEM)
SM = pl.BlockSpec(memory_space=pltpu.SMEM)


def shape(*dims, kind=F32):
    return jax.ShapeDtypeStruct(dims, kind)


def per_device(features, tile_rows, tile_cols, tile_values, weight_in, weight_out, cotangent):
    ints, floats = pl.pallas_call(
        tables_kernel,
        out_shape=(shape(8, 128, kind=jnp.int32), shape(8, 128)),
        in_specs=[VM, VM],
        out_specs=(VM, VM),
        scratch_shapes=[pltpu.VMEM((8, 128), jnp.int32)],
        name="tables",
    )(tile_rows.reshape(1, SLOTS), tile_cols.reshape(1, SLOTS))
    outs_shape = (shape(256, 256), shape(128, 256), shape(256, 256))
    outs = pl.pallas_call(
        step_kernel,
        out_shape=outs_shape,
        in_specs=[SM, SM, ANY, ANY, ANY, VM, VM],
        out_specs=(VM, VM, VM),
        scratch_shapes=[pltpu.VMEM(dims, kind) for dims, kind in SCRATCH.values()]
        + [
            pltpu.SemaphoreType.DMA((COPIES,)),
            pltpu.SemaphoreType.DMA((COPIES,)),
            pltpu.SemaphoreType.DMA((SLOTS // CHUNK + 2,)),
        ],
        compiler_params=pltpu.CompilerParams(
            collective_id=0, has_side_effects=True, vmem_limit_bytes=VMEM_LIMIT),
        name="step",
    )(ints, floats, features.T, cotangent.reshape(2, 128, 256), tile_values.reshape(SLOTS, 128, 128),
      weight_in, weight_out)
    return pl.pallas_call(
        finish_kernel, out_shape=outs_shape, in_specs=[VM] * 3, out_specs=(VM,) * 3, name="finish",
    )(*outs)


def solution(mesh):
    return jax.shard_map(
        per_device,
        mesh=mesh,
        in_specs=(
            P("col", "row"),
            P("row", "col", None),
            P("row", "col", None),
            P("row", "col", None, None, None),
            P(),
            P(),
            P(("col", "row"), None),
        ),
        out_specs=(P(("col", "row"), None), P(), P()),
        check_vma=False,
    )
```

```python
import heapq
import math
import types

import jax
import jax.numpy as jnp
from jax import lax
from jax.experimental import pallas as pl
from jax.experimental.pallas import tpu as pltpu
from jax.sharding import PartitionSpec as P

MESH = pl.DeviceIdType.MESH
F32 = jnp.float32
BF16 = jnp.bfloat16
VMEM_LIMIT = 67043328
CHUNK = 8
SLOTS = 80
TROWS = 32
TCOLS = 16
COPIES = 320


def split(v):
    hi = v.astype(BF16)
    return hi, (v - hi.astype(F32)).astype(BF16)


def dot16(a, b, dims=(((1,), (0,)), ((), ()))):
    return lax.dot_general(a, b, dims, preferred_element_type=F32)


def dot3(a, b, dims=(((1,), (0,)), ((), ()))):
    ah, al = split(a)
    bh, bl = split(b)
    return dot16(ah, bl, dims) + dot16(al, bh, dims) + dot16(ah, bh, dims)


class Copy:
    def __init__(self, src, dst, axis, shift):
        self.src, self.dst, self.axis, self.shift = src, dst, axis, shift
        self.bytes = 4 * math.prod(src.shape)
        self.copy = self.arrival = None


RATE = {"x": 45e3, "y": 45e3, "z": 45e3, "core": 250e3}
DELAY = {"x": 1.6, "y": 1.6, "z": 1.6, "core": 1.0}
WINDOW = 1.5


class Tick:
    def __init__(self, net, spent, level):
        net.now += spent
        self.arrival = net.now + level * 1e-3


class Net:
    def __init__(self, send_sems, recv_sems):
        self.send_sems, self.recv_sems = send_sems, recv_sems
        self.copies = []
        i, j = lax.axis_index("row"), lax.axis_index("col")
        self.x, self.core = i // 2, lax.rem(i, 2)
        self.z, self.y = j // 4, lax.rem(j, 4)
        self.i, self.j = i, j
        self.active, self.pending, self.free = [], {}, {}
        self.now, self.count = 0.0, 0

    def pos(self, axis):
        return {"x": self.x, "y": self.y, "z": self.z}[axis]

    def at(self, axis, shift):
        return lax.rem(self.pos(axis) + (shift + 4), 4)

    def peer(self, axis, shift):
        if axis == "core":
            return (self.x * 2 + 1 - self.core, self.j)
        p = self.at(axis, shift)
        if axis == "x":
            return (p * 2 + self.core, self.j)
        if axis == "y":
            return (self.i, self.z * 4 + p)
        return (self.i, p * 4 + self.y)

    def barrier(self, axes):
        sem = pltpu.get_barrier_semaphore()
        n = 0
        for axis in axes:
            for shift in (1,) if axis == "core" else (1, -1, 2):
                pl.semaphore_signal(sem, inc=1, device_id=self.peer(axis, shift), device_id_type=MESH)
                n += 1
        pl.semaphore_wait(sem, n)

    def send(self, src, dst, axis, shift=1, level=5):
        copy = Copy(src, dst, axis, shift)
        self.count += 1
        link = (axis, 1 if shift == 2 else shift)
        heapq.heappush(self.pending.setdefault(link, []), (level, self.count, copy))
        return copy

    def pump(self):
        for link, heap in self.pending.items():
            while heap and self.free.get(link, 0.0) < self.now + WINDOW:
                one = heapq.heappop(heap)[2]
                k = len(self.copies)
                one.copy = pltpu.make_async_remote_copy(
                    src_ref=one.src,
                    dst_ref=one.dst,
                    send_sem=self.send_sems.at[k],
                    recv_sem=self.recv_sems.at[k],
                    device_id=self.peer(one.axis, one.shift),
                    device_id_type=MESH,
                )
                one.copy.start()
                self.copies.append(one.copy)
                end = max(self.now, self.free.get(link, 0.0)) + one.bytes / RATE[one.axis]
                self.free[link] = end
                one.arrival = end + DELAY[one.axis] * (1.5 if one.shift == 2 else 1)

    def spawn(self, gen):
        self.active.append([gen, None])

    def run(self):
        while True:
            moved = True
            while moved:
                moved = False
                for entry in list(self.active):
                    if entry[1] is None or (callable(entry[1]) and entry[1]()):
                        moved = True
                        self.step(entry)
            self.pump()
            waits = [e for e in self.active if not callable(e[1]) and e[1].arrival is not None]
            if waits:
                entry = min(waits, key=lambda e: e[1].arrival)
                self.now = max(self.now, entry[1].arrival)
                if isinstance(entry[1], Copy):
                    entry[1].copy.wait_recv()
                self.step(entry)
            elif any(self.pending.values()):
                self.now = min(self.free.get(link, 0.0) for link, heap in self.pending.items() if heap)
                self.now -= WINDOW / 2
            else:
                break
        assert not self.active
        for copy in self.copies:
            copy.wait_send()

    def step(self, entry):
        try:
            entry[1] = next(entry[0])
        except StopIteration:
            self.active.remove(entry)


def arrive(copy, have=None):
    yield copy
    if have is not None:
        have()


def ag_unit(net, axis, src, ref, have, way, level=5):
    p = net.at(axis, 0)
    near = net.send(src, ref(p), axis, way, level)
    other = net.send(src, ref(p), axis, -way, level)

    def chain():
        yield near
        pos = net.at(axis, -way)
        onward = net.send(ref(pos), ref(pos), axis, way, level)
        have(pos)
        yield onward
        have(net.at(axis, 2))

    net.spawn(chain())
    net.spawn(arrive(other, lambda: have(net.at(axis, way))))


def rs_unit(net, axis, part, ready, stage, emit, way, level=5, after=None):
    r, m, q = (stage(k) for k in range(3))
    box = []
    after = level if after is None else after

    def near():
        yield lambda: ready[-way]
        box.append(net.send(part(net.at(axis, -way)), q, axis, -way, level))

    def far():
        yield lambda: ready[2]
        first = net.send(part(net.at(axis, 2)), r, axis, way, level)
        yield first
        yield lambda: ready[way]
        r[...] = r[...] + part(net.at(axis, way))[...]
        yield net.send(r, m, axis, way, after)
        yield lambda: box
        yield box[0]
        yield lambda: ready[0]
        emit(part(net.at(axis, 0))[...] + (m[...] + q[...]))

    net.spawn(far())
    net.spawn(near())


def gather_direct(net, axis, src, dst, level=0):
    copies = [net.send(src, dst.at[net.at(axis, 0)], axis, d, level) for d in (2, 1, -1)]
    for copy in copies[1:] + copies[:1]:
        yield copy


def reduce_direct(net, axis, terms, land, level=0):
    copies = [net.send(terms.at[net.at(axis, d)], land.at[k], axis, d, level) for k, d in enumerate((2, 1, -1))]
    for copy in copies[1:] + copies[:1]:
        yield copy


ALL = {0: True, 1: True, 2: True, -1: True}
SHIFTS = (2, 1, -1, 0)
WAYS = (1, -1)


def rs_plane(net, tiles, stage_one, middle, stage_two, out, done, lanes=slice(None), base=0):
    for part, (first, second) in enumerate((("z", "y"), ("y", "z"))):
        for u, way in enumerate(WAYS):
            ready = {d: False for d in SHIFTS}
            for k, d in enumerate((2, way, -way, 0)):
                pos2 = net.at(second, d)

                def term(pos1, pos2=pos2, part=part, u=u, first=first):
                    block = pos1 * 4 + pos2 if first == "z" else pos2 * 4 + pos1
                    return tiles.at[2 * block + part, pl.ds(u * 64, 64), :]

                def land(s, part=part, u=u, k=k):
                    return stage_one.at[part, k, u, s]

                def emit(value, part=part, u=u, pos2=pos2, d=d, ready=ready):
                    middle[part, pos2, u] = value
                    ready[d] = True

                rs_unit(net, first, term, ALL, land, emit, way, level=base + 3 + k, after=base + 2)

            def term2(pos, part=part, u=u):
                return middle.at[part, pos, u]

            def land2(s, part=part, u=u):
                return stage_two.at[part, u, s]

            def emit2(value, part=part, u=u):
                out[part * 128 + u * 64 : part * 128 + u * 64 + 64, lanes] = value
                done.append((part, u))

            rs_unit(net, second, term2, ready, land2, emit2, way, level=base + 1)


def tables_kernel(rows_ref, cols_ref, int_ref, float_ref, pad):
    pad[0:1, :] = jnp.full((1, 128), TROWS, jnp.int32)
    pad[1:2, :] = jnp.zeros((1, 128), jnp.int32)
    pad[0:1, :SLOTS] = rows_ref[...]
    pad[1:2, :SLOTS] = cols_ref[...]
    lane = lax.broadcasted_iota(jnp.int32, (128, 128), 1)
    line = lax.broadcasted_iota(jnp.int32, (128, 128), 0)

    def wide(v):
        return jnp.broadcast_to(v, (128, 128))

    def count(v):
        return jnp.sum(v, axis=0, keepdims=True)

    row, col = pad[0:1, :], pad[1:2, :]
    used = row < TROWS
    for major, minor, size, k in ((row, col, TROWS, 0), (col, row, TCOLS, 3)):
        major, minor = jnp.where(used, major, size), jnp.where(used, minor, 0)
        key = wide(major * 64 + minor)
        key_t = jnp.transpose(key)
        before = (key_t < key) | ((key_t == key) & (line < lane))
        rank_t = jnp.transpose(wide(count(before.astype(jnp.int32))))
        here = rank_t == lane
        order = count(jnp.where(here, line, 0))
        sorted_key = count(jnp.where(here, key_t, 0))
        group = sorted_key // 64
        group_t = jnp.transpose(wide(group))
        found = count((group_t == lane).astype(jnp.int32)) > 0
        last = jnp.where(found, count((group_t <= lane).astype(jnp.int32)), 0)
        int_ref[k : k + 1, :] = order
        int_ref[k + 1 : k + 2, :] = sorted_key - group * 64
        int_ref[k + 2 : k + 3, :] = last
        same = count(((group_t == wide(group)) & (line + 1 == lane)).astype(jnp.int32))
        float_ref[k : k + 1, :] = same.astype(F32)


SCRATCH = {
    "buf": ((2, CHUNK, 128, 128), F32),
    "acat": ((SLOTS, 128, 256), BF16),
    "atc": ((SLOTS, 128, 256), BF16),
    "sums_f": ((SLOTS + 1, 128, 128), F32),
    "sums_a": ((SLOTS + 1, 128, 256), F32),
    "xt": ((8, 16, 2048), F32),
    "xh": ((16, 128, 128), BF16),
    "xl": ((16, 128, 128), BF16),
    "cots": ((32, 128, 256), F32),
    "s2_0": ((16, 128, 128), F32),
    "s2_1": ((16, 128, 128), F32),
    "fwd1": ((32, 128, 128), F32),
    "fwd2": ((2, 32, 128, 128), F32),
    "adj": ((16, 128, 256), F32),
    "a1": ((2, 4, 2, 3, 64, 128), F32),
    "m1": ((2, 4, 2, 64, 128), F32),
    "b1": ((2, 2, 3, 64, 128), F32),
    "a2": ((2, 2, 4, 2, 3, 64, 128), F32),
    "m2": ((2, 2, 4, 2, 64, 128), F32),
    "b2": ((2, 2, 2, 3, 64, 128), F32),
    "c3": ((2, 4, 128, 256), F32),
    "m3": ((2, 4, 128, 256), F32),
    "d3": ((2, 3, 128, 256), F32),
    "s": ((256, 128), F32),
    "d": ((256, 256), F32),
    "h": ((256, 256), F32),
    "p": ((256, 256), F32),
    "g": ((2, 384, 128), F32),
    "ge": ((384, 128), F32),
    "g1": ((4, 96, 128), F32),
    "gf": ((3, 96, 128), F32),
    "gs": ((96, 128), F32),
    "g2": ((4, 96, 128), F32),
    "gz": ((4, 96, 128), F32),
    "gy": ((4, 96, 128), F32),
    "gsib": ((4, 96, 128), F32),
}
BLOCK = 8
UNROLL = 4


def step_kernel(int_ref, float_ref, feat_ref, cot_ref, tiles_ref, win_ref, wout_ref,
                out_ref, gin_ref, gout_ref, *scratch):
    w = types.SimpleNamespace(**dict(zip(SCRATCH, scratch)))
    send_sems, recv_sems, local_sems = scratch[len(SCRATCH):]
    chunks = SLOTS // CHUNK

    def chunk_copy(k):
        return pltpu.make_async_copy(tiles_ref.at[pl.ds(k * CHUNK, CHUNK)], w.buf.at[k % 2], local_sems.at[k])

    net = Net(send_sems, recv_sems)
    loads = [chunk_copy(k) for k in range(chunks)]
    loads[0].start()
    loads[1].start()
    own_x = pltpu.make_async_copy(feat_ref, w.xt.at[net.i], local_sems.at[chunks])
    own_c = pltpu.make_async_copy(
        cot_ref, w.cots.at[pl.ds(net.j * 2, 2)], local_sems.at[chunks + 1])
    own_x.start()
    own_c.start()
    w.sums_f[0] = jnp.zeros_like(w.sums_f[0])
    w.sums_a[0] = jnp.zeros_like(w.sums_a[0])
    net.barrier(("x", "core", "y", "z"))
    seen = {"x": 0, "cot": 0, 0: 0, 1: 0}
    done = {}

    def saw(name):
        seen[name] += 1

    def row_gather(name, src, ref_of, own_src, own_dst, level=0):
        for u, way in enumerate(WAYS):

            def ref(pos, u=u):
                return ref_of(pos * 2 + net.core, u)

            def have(pos, ref=ref):
                saw(name)
                net.spawn(arrive(net.send(ref(pos), ref(pos), "core"), lambda: saw(name)))

            ag_unit(net, "x", src(u), ref, have, way, level)
        net.spawn(arrive(net.send(own_src, own_dst, "core"), lambda: saw(name)))

    def halves(u):
        return pl.ds(u * 8, 8)

    row_gather("x", lambda u: feat_ref.at[halves(u), :], lambda i, u: w.xt.at[i, halves(u), :],
               feat_ref, w.xt.at[net.i])

    for part, (first, second) in enumerate((("y", "z"), ("z", "y"))):
        for u, way in enumerate(WAYS):
            rows = pl.ds(u * 64, 64)
            src = cot_ref.at[part, rows, :]

            def ref(pos1, pos2, rows=rows, first=first, part=part):
                block = pos1 + pos2 * 4 if first == "y" else pos1 * 4 + pos2
                return w.cots.at[2 * block + part, rows, :]

            def start_second(pos1, src=None, ref=ref, second=second, way=way):
                src = ref(pos1, net.at(second, 0)) if src is None else src
                ag_unit(net, second, src, lambda pos2: ref(pos1, pos2), lambda pos: saw("cot"), way, -1)

            def have_one(pos1, start_second=start_second):
                saw("cot")
                start_second(pos1)

            ag_unit(net, first, src, lambda pos1, ref=ref, second=second: ref(pos1, net.at(second, 0)),
                    have_one, way, level=-2)
            start_second(net.at(first, 0), src)

    def sums(base, k, lhs, product, store):
        def body(q, _):
            acc = None
            for v in range(UNROLL):
                n = base + q * UNROLL + v
                prev = store(n)[...] if acc is None else acc
                acc = prev * float_ref[k, n] + product(lhs[int_ref[k, n]], int_ref[k + 1, n])
                store(n + 1)[...] = acc
            return 0

        lax.fori_loop(0, BLOCK // UNROLL, body, 0)

    def pick(k, count, load, out):
        def body(r, _):
            out[r] = load(int_ref[k + 2, r])
            return 0

        lax.fori_loop(0, count, body, 0)

    def wide_product(values):
        def product(left, n):
            h, l = split(values[n])
            return dot16(left, jnp.concatenate([h, h], axis=0)) + dot16(left[:, :128], l)

        return product

    def narrow(left, h, l):
        pair = jnp.concatenate([h, l], axis=1)
        res = dot16(left, jnp.concatenate([pair, pair], axis=0))
        return res[:, :128] + res[:, 128:]

    def tiles():
        for k in range(chunks):
            loads[k].wait()

            def body(n, _, k=k):
                h, l = split(w.buf[k % 2, n])
                w.acat[k * CHUNK + n] = jnp.concatenate([h, l], axis=1)
                return 0

            lax.fori_loop(0, CHUNK, body, 0)
            if k + 2 < chunks:
                loads[k + 2].start()
            yield Tick(net, 0.5, 0)
        done["acat"] = True
        for k in range(chunks):

            def turn(n, _, k=k):
                t = k * CHUNK + n
                both = w.acat[t]
                w.atc[t] = jnp.concatenate([jnp.transpose(both[:, :128]), jnp.transpose(both[:, 128:])], axis=1)
                return 0

            lax.fori_loop(0, CHUNK, turn, 0)
            yield Tick(net, 0.6, 5)
        done["atc"] = True

    def first_layer():
        yield lambda: seen["x"] == 13 and done.get("acat")
        own_x.wait()

        def split_x(c, _):
            piece = w.xt[:, :, pl.ds(pl.multiple_of(c * 128, 128), 128)].reshape(128, 128)
            h, l = split(jnp.transpose(piece))
            w.xh[c] = h
            w.xl[c] = l
            return 0

        lax.fori_loop(0, 16, split_x, 0)
        yield Tick(net, 1.0, 0)
        for base in range(0, SLOTS, BLOCK):
            sums(base, 0, w.acat, lambda left, n: narrow(left, w.xh[n], w.xl[n]), lambda n: w.sums_f.at[n])
            yield Tick(net, 0.6, 0)
        pick(0, 32, lambda n: w.sums_f[n], w.fwd1)
        net.now += 0.5
        parts = []
        rs_plane(net, w.fwd1, w.a1, w.m1, w.b1, w.s, parts)
        yield lambda: len(parts) == 4
        pre = dot3(w.s[...], win_ref[...])
        hidden = pre * (1.0 / (1.0 + jnp.exp(-pre)))
        w.p[...] = pre
        w.h[...] = hidden
        for f in range(2):
            s2 = (w.s2_0, w.s2_1)[f]
            mine = s2.at[pl.ds(net.i * 2, 2)]
            mine[...] = dot3(hidden, wout_ref[:, f * 128 : f * 128 + 128]).reshape(2, 128, 128)
            net.now += 0.6
            row_gather(f, lambda u, s2=s2: s2.at[net.i * 2 + u], lambda i, u, s2=s2: s2.at[i * 2 + u], mine, mine, f)
            net.pump()
        done["pre"] = True
        for f in range(2):
            yield lambda: seen[f] == 13
            s2 = (w.s2_0, w.s2_1)[f]
            for base in range(0, SLOTS, BLOCK):
                sums(base, 0, w.acat, lambda left, n: narrow(left, *split(s2[n])), lambda n: w.sums_f.at[n])
                yield Tick(net, 0.6, 1)
            pick(0, 32, lambda n: w.sums_f[n], w.fwd2.at[f])
            net.now += 0.5
            rs_plane(net, w.fwd2.at[f], w.a2.at[f], w.m2.at[f], w.b2.at[f], out_ref, [],
                     slice(f * 128, f * 128 + 128), 6 * f)

    def adjoint():
        yield lambda: seen["cot"] == 60 and done.get("atc")
        own_c.wait()
        for base in range(0, SLOTS, BLOCK):
            sums(base, 3, w.atc, wide_product(w.cots), lambda n: w.sums_a.at[n])
            yield Tick(net, 0.9, 2)
        pick(3, 16, lambda n: w.sums_a[n], w.adj)
        net.now += 0.5
        parts = []
        for u, way in enumerate(WAYS):
            ready = {d: False for d in SHIFTS}
            for k, d in enumerate((2, way, -way, 0)):
                pos = net.at("x", d)

                def cores(u=u, k=k, d=d, pos=pos, ready=ready):
                    land = w.c3.at[u, k]
                    yield net.send(w.adj.at[(pos * 2 + 1 - net.core) * 2 + u], land, "core", 1, k)
                    w.m3[u, pos] = w.adj[(pos * 2 + net.core) * 2 + u] + land[...]
                    ready[d] = True

                net.spawn(cores())

            def emit_d(value, u=u):
                w.d[pl.ds(u * 128, 128), :] = value
                parts.append(u)

            rs_unit(net, "x", lambda pos, u=u: w.m3.at[u, pos], ready, lambda k, u=u: w.d3.at[u, k], emit_d, way, 0.5)
        yield lambda: len(parts) == 2 and done.get("pre")
        net.pump()
        d = w.d[...]
        pre = w.p[...]
        sg = 1.0 / (1.0 + jnp.exp(-pre))
        d_pre = dot3(d, wout_ref[...], (((1,), (1,)), ((), ()))) * sg * (1.0 + pre * (1.0 - sg))
        grad_in = dot3(jnp.transpose(w.s[...]), d_pre)
        grad_out = dot3(jnp.transpose(w.h[...]), d)
        for c in range(2):
            lanes = slice(c * 128, c * 128 + 128)
            w.g[c, pl.ds(0, 128), :] = grad_in[:, lanes]
            w.g[c, pl.ds(128, 256), :] = grad_out[:, lanes]
        net.now += 2.0
        yield net.send(w.g.at[1 - net.core], w.ge, "core", 1, 0)
        w.g1[...] = (w.g[net.core] + w.ge[...]).reshape(w.g1.shape)

        def total(terms, own, land):
            return (terms[own] + land[0]) + (land[1] + land[2])

        yield from reduce_direct(net, "x", w.g1, w.gf)
        w.gs[...] = total(w.g1, net.x, w.gf)
        for axis, land in (("y", w.g2), ("z", w.gz)):
            land[net.pos(axis)] = w.gs[...]
            yield from gather_direct(net, axis, land.at[net.pos(axis)], land)
            w.gs[...] = (land[0] + land[1]) + (land[2] + land[3])
        w.gy[net.x] = w.gs[...]
        yield from gather_direct(net, "x", w.gs, w.gy)
        yield net.send(w.gy, w.gsib, "core", 1, 0)
        mine, other = w.gy[...].reshape(384, 128), w.gsib[...].reshape(384, 128)
        first = net.core == 0
        low = jnp.where(first, mine, other)
        high = jnp.where(first, other, mine)
        gin_ref[:, :128] = low[:128]
        gin_ref[:, 128:] = high[:128]
        gout_ref[:, :128] = low[128:]
        gout_ref[:, 128:] = high[128:]

    net.spawn(tiles())
    net.spawn(first_layer())
    net.spawn(adjoint())
    net.run()


def finish_kernel(a_ref, b_ref, c_ref, out_a, out_b, out_c):
    out_a[...] = a_ref[...]
    out_b[...] = b_ref[...]
    out_c[...] = c_ref[...]


ANY = pl.BlockSpec(memory_space=pl.ANY)
VM = pl.BlockSpec(memory_space=pltpu.VMEM)
SM = pl.BlockSpec(memory_space=pltpu.SMEM)


def shape(*dims, kind=F32):
    return jax.ShapeDtypeStruct(dims, kind)


def per_device(features, tile_rows, tile_cols, tile_values, weight_in, weight_out, cotangent):
    ints, floats = pl.pallas_call(
        tables_kernel,
        out_shape=(shape(8, 128, kind=jnp.int32), shape(8, 128)),
        in_specs=[VM, VM],
        out_specs=(VM, VM),
        scratch_shapes=[pltpu.VMEM((8, 128), jnp.int32)],
        name="tables",
    )(tile_rows.reshape(1, SLOTS), tile_cols.reshape(1, SLOTS))
    outs_shape = (shape(256, 256), shape(128, 256), shape(256, 256))
    outs = pl.pallas_call(
        step_kernel,
        out_shape=outs_shape,
        in_specs=[SM, SM, ANY, ANY, ANY, VM, VM],
        out_specs=(VM, VM, VM),
        scratch_shapes=[pltpu.VMEM(dims, kind) for dims, kind in SCRATCH.values()]
        + [
            pltpu.SemaphoreType.DMA((COPIES,)),
            pltpu.SemaphoreType.DMA((COPIES,)),
            pltpu.SemaphoreType.DMA((SLOTS // CHUNK + 2,)),
        ],
        compiler_params=pltpu.CompilerParams(
            collective_id=0, has_side_effects=True, vmem_limit_bytes=VMEM_LIMIT),
        name="step",
    )(ints, floats, features.T, cotangent.reshape(2, 128, 256), tile_values.reshape(SLOTS, 128, 128),
      weight_in, weight_out)
    return pl.pallas_call(
        finish_kernel, out_shape=outs_shape, in_specs=[VM] * 3, out_specs=(VM,) * 3, name="finish",
    )(*outs)


def solution(mesh):
    return jax.shard_map(
        per_device,
        mesh=mesh,
        in_specs=(
            P("col", "row"),
            P("row", "col", None),
            P("row", "col", None),
            P("row", "col", None, None, None),
            P(),
            P(),
            P(("col", "row"), None),
        ),
        out_specs=(P(("col", "row"), None), P(), P()),
        check_vma=False,
    )
```

```python
import heapq
import math
import types

import jax
import jax.numpy as jnp
from jax import lax
from jax.experimental import pallas as pl
from jax.experimental.pallas import tpu as pltpu
from jax.sharding import PartitionSpec as P

MESH = pl.DeviceIdType.MESH
F32 = jnp.float32
BF16 = jnp.bfloat16
VMEM_LIMIT = 67043328
CHUNK = 8
SLOTS = 80
TROWS = 32
TCOLS = 16
COPIES = 307
SIZES = tuple(k * 1024 for k in (32, 48, 64, 128, 192))


def split(v):
    hi = v.astype(BF16)
    return hi, (v - hi.astype(F32)).astype(BF16)


def dot16(a, b, dims=(((1,), (0,)), ((), ()))):
    return lax.dot_general(a, b, dims, preferred_element_type=F32)


def dot3(a, b, dims=(((1,), (0,)), ((), ()))):
    ah, al = split(a)
    bh, bl = split(b)
    return dot16(ah, bl, dims) + dot16(al, bh, dims) + dot16(ah, bh, dims)


class Copy:
    def __init__(self, src, dst, axis, shift):
        self.src, self.dst, self.axis, self.shift = src, dst, axis, shift
        self.bytes = 4 * math.prod(src.shape)
        self.copy = self.arrival = None


RATE = {"x": 45e3, "y": 45e3, "z": 45e3, "core": 250e3}
DELAY = {"x": 1.6, "y": 1.6, "z": 1.6, "core": 1.0}
WINDOW = 3.0


class Tick:
    def __init__(self, net, spent, level):
        net.now += spent
        self.arrival = net.now + level * 1e-3


class Net:
    def __init__(self, send_sems, recv_sems):
        self.send_sems, self.recv_sems = send_sems, recv_sems
        self.copies, self.sent = [], {}
        i, j = lax.axis_index("row"), lax.axis_index("col")
        self.x, self.core = i // 2, lax.rem(i, 2)
        self.z, self.y = j // 4, lax.rem(j, 4)
        self.i, self.j = i, j
        self.active, self.pending, self.free = [], {}, {}
        self.now, self.count = 0.0, 0

    def pos(self, axis):
        return {"x": self.x, "y": self.y, "z": self.z}[axis]

    def at(self, axis, shift):
        return lax.rem(self.pos(axis) + (shift + 4), 4)

    def peer(self, axis, shift):
        if axis == "core":
            return (self.x * 2 + 1 - self.core, self.j)
        p = self.at(axis, shift)
        if axis == "x":
            return (p * 2 + self.core, self.j)
        if axis == "y":
            return (self.i, self.z * 4 + p)
        return (self.i, p * 4 + self.y)

    def barrier(self, axes):
        sem = pltpu.get_barrier_semaphore()
        n = 0
        for axis in axes:
            for shift in (1,) if axis == "core" else (1, -1, 2):
                pl.semaphore_signal(sem, inc=1, device_id=self.peer(axis, shift), device_id_type=MESH)
                n += 1
        pl.semaphore_wait(sem, n)

    def send(self, src, dst, axis, shift=1, level=5):
        copy = Copy(src, dst, axis, shift)
        self.count += 1
        link = (axis, 1 if shift == 2 else shift)
        heapq.heappush(self.pending.setdefault(link, []), (level, self.count, copy))
        return copy

    def pump(self):
        for link, heap in self.pending.items():
            while heap and self.free.get(link, 0.0) < self.now + WINDOW:
                one = heapq.heappop(heap)[2]
                k = len(self.copies)
                one.copy = pltpu.make_async_remote_copy(
                    src_ref=one.src,
                    dst_ref=one.dst,
                    send_sem=self.send_sems.at[SIZES.index(one.bytes)],
                    recv_sem=self.recv_sems.at[k],
                    device_id=self.peer(one.axis, one.shift),
                    device_id_type=MESH,
                )
                one.copy.start()
                self.copies.append(one.copy)
                self.sent[one.bytes] = self.sent.get(one.bytes, 0) + one.bytes
                end = max(self.now, self.free.get(link, 0.0)) + one.bytes / RATE[one.axis]
                self.free[link] = end
                one.arrival = end + DELAY[one.axis] * (1.5 if one.shift == 2 else 1)

    def spawn(self, gen):
        self.active.append([gen, None])

    def run(self, whole):
        while True:
            moved = True
            while moved:
                moved = False
                for entry in list(self.active):
                    if entry[1] is None or (callable(entry[1]) and entry[1]()):
                        moved = True
                        self.step(entry)
            self.pump()
            waits = [e for e in self.active if not callable(e[1]) and e[1].arrival is not None]
            if waits:
                entry = min(waits, key=lambda e: e[1].arrival)
                self.now = max(self.now, entry[1].arrival)
                if isinstance(entry[1], Copy):
                    entry[1].copy.wait_recv()
                self.step(entry)
            elif any(self.pending.values()):
                self.now = min(self.free.get(link, 0.0) for link, heap in self.pending.items() if heap)
                self.now -= WINDOW / 2
            else:
                break
        assert not self.active
        assert len(self.copies) == COPIES
        for size, total in self.sent.items():
            unit = 128 if total % (128 * 1024) == 0 else 64
            span = whole[unit].at[pl.ds(0, total // (unit * 1024))]
            assert 4 * math.prod(span.shape) * (1 if unit == 128 else 0.5) == total
            pltpu.make_async_remote_copy(
                src_ref=span,
                dst_ref=span,
                send_sem=self.send_sems.at[SIZES.index(size)],
                recv_sem=self.recv_sems.at[0],
                device_id=self.peer("core", 1),
                device_id_type=MESH,
            ).wait_send()

    def step(self, entry):
        try:
            entry[1] = next(entry[0])
        except StopIteration:
            self.active.remove(entry)


def arrive(copy, have=None):
    yield copy
    if have is not None:
        have()


def ag_unit(net, axis, src, ref, have, way, level=5):
    p = net.at(axis, 0)
    near = net.send(src, ref(p), axis, way, level)
    other = net.send(src, ref(p), axis, -way, level)

    def chain():
        yield near
        pos = net.at(axis, -way)
        onward = net.send(ref(pos), ref(pos), axis, way, level)
        have(pos)
        yield onward
        have(net.at(axis, 2))

    net.spawn(chain())
    net.spawn(arrive(other, lambda: have(net.at(axis, way))))


def rs_unit(net, axis, part, ready, stage, emit, way, level=5, after=None):
    r, m, q = (stage(k) for k in range(3))
    box = []
    after = level if after is None else after

    def near():
        yield lambda: ready[-way]
        box.append(net.send(part(net.at(axis, -way)), q, axis, -way, level))

    def far():
        yield lambda: ready[2]
        first = net.send(part(net.at(axis, 2)), r, axis, way, level)
        yield first
        yield lambda: ready[way]
        r[...] = r[...] + part(net.at(axis, way))[...]
        yield net.send(r, m, axis, way, after)
        yield lambda: box
        yield box[0]
        yield lambda: ready[0]
        emit(part(net.at(axis, 0))[...] + (m[...] + q[...]))

    net.spawn(far())
    net.spawn(near())


def gather_direct(net, axis, src, dst, level=0):
    copies = [net.send(src, dst.at[net.at(axis, 0)], axis, d, level) for d in (2, 1, -1)]
    for copy in copies[1:] + copies[:1]:
        yield copy


def reduce_direct(net, axis, terms, land, level=0):
    copies = [net.send(terms.at[net.at(axis, d)], land.at[k], axis, d, level) for k, d in enumerate((2, 1, -1))]
    for copy in copies[1:] + copies[:1]:
        yield copy


ALL = {0: True, 1: True, 2: True, -1: True}
SHIFTS = (2, 1, -1, 0)
WAYS = (1, -1)


def rs_plane(net, tiles, stage_one, middle, stage_two, out, done, lanes=slice(None), base=0):
    for part, (first, second) in enumerate((("z", "y"), ("y", "z"))):
        for u, way in enumerate(WAYS):
            ready = {d: False for d in SHIFTS}
            for k, d in enumerate((2, way, -way, 0)):
                pos2 = net.at(second, d)

                def term(pos1, pos2=pos2, part=part, u=u, first=first):
                    block = pos1 * 4 + pos2 if first == "z" else pos2 * 4 + pos1
                    return tiles.at[2 * block + part, pl.ds(u * 64, 64), :]

                def land(s, part=part, u=u, k=k):
                    return stage_one.at[part, k, u, s]

                def emit(value, part=part, u=u, pos2=pos2, d=d, ready=ready):
                    middle[part, pos2, u] = value
                    ready[d] = True

                rs_unit(net, first, term, ALL, land, emit, way, level=base + 3 + k, after=base + 2)

            def term2(pos, part=part, u=u):
                return middle.at[part, pos, u]

            def land2(s, part=part, u=u):
                return stage_two.at[part, u, s]

            def emit2(value, part=part, u=u):
                out[part * 128 + u * 64 : part * 128 + u * 64 + 64, lanes] = value
                done.append((part, u))

            rs_unit(net, second, term2, ready, land2, emit2, way, level=base + 1)


def tables_kernel(rows_ref, cols_ref, int_ref, float_ref, pad):
    pad[0:1, :] = jnp.full((1, 128), TROWS, jnp.int32)
    pad[1:2, :] = jnp.zeros((1, 128), jnp.int32)
    pad[0:1, :SLOTS] = rows_ref[...]
    pad[1:2, :SLOTS] = cols_ref[...]
    lane = lax.broadcasted_iota(jnp.int32, (128, 128), 1)
    line = lax.broadcasted_iota(jnp.int32, (128, 128), 0)

    def wide(v):
        return jnp.broadcast_to(v, (128, 128))

    def count(v):
        return jnp.sum(v, axis=0, keepdims=True)

    row, col = pad[0:1, :], pad[1:2, :]
    used = row < TROWS
    for major, minor, size, k in ((row, col, TROWS, 0), (col, row, TCOLS, 3)):
        major, minor = jnp.where(used, major, size), jnp.where(used, minor, 0)
        key = wide(major * 64 + minor)
        key_t = jnp.transpose(key)
        before = (key_t < key) | ((key_t == key) & (line < lane))
        rank_t = jnp.transpose(wide(count(before.astype(jnp.int32))))
        here = rank_t == lane
        order = count(jnp.where(here, line, 0))
        sorted_key = count(jnp.where(here, key_t, 0))
        group = sorted_key // 64
        group_t = jnp.transpose(wide(group))
        found = count((group_t == lane).astype(jnp.int32)) > 0
        last = jnp.where(found, count((group_t <= lane).astype(jnp.int32)), 0)
        int_ref[k : k + 1, :] = order
        int_ref[k + 1 : k + 2, :] = sorted_key - group * 64
        int_ref[k + 2 : k + 3, :] = last
        same = count(((group_t == wide(group)) & (line + 1 == lane)).astype(jnp.int32))
        float_ref[k : k + 1, :] = same.astype(F32)


SCRATCH = {
    "buf": ((SLOTS, 128, 128), F32),
    "acat": ((SLOTS, 128, 256), BF16),
    "atc": ((SLOTS, 128, 256), BF16),
    "sums_f": ((SLOTS + 1, 128, 128), F32),
    "sums_a": ((SLOTS + 1, 128, 256), F32),
    "xt": ((8, 16, 2048), F32),
    "xh": ((16, 128, 128), BF16),
    "xl": ((16, 128, 128), BF16),
    "cots": ((32, 128, 256), F32),
    "s2_0": ((16, 128, 128), F32),
    "s2_1": ((16, 128, 128), F32),
    "fwd1": ((32, 128, 128), F32),
    "fwd2": ((2, 32, 128, 128), F32),
    "adj": ((16, 128, 256), F32),
    "a1": ((2, 4, 2, 3, 64, 128), F32),
    "m1": ((2, 4, 2, 64, 128), F32),
    "b1": ((2, 2, 3, 64, 128), F32),
    "a2": ((2, 2, 4, 2, 3, 64, 128), F32),
    "m2": ((2, 2, 4, 2, 64, 128), F32),
    "b2": ((2, 2, 2, 3, 64, 128), F32),
    "c3": ((2, 4, 128, 256), F32),
    "m3": ((2, 4, 128, 256), F32),
    "d3": ((2, 3, 128, 256), F32),
    "s": ((256, 128), F32),
    "d": ((256, 256), F32),
    "h": ((256, 256), F32),
    "p": ((256, 256), F32),
    "g": ((2, 384, 128), F32),
    "ge": ((384, 128), F32),
    "g1": ((4, 96, 128), F32),
    "gf": ((3, 96, 128), F32),
    "gs": ((96, 128), F32),
    "g2": ((4, 96, 128), F32),
    "gz": ((4, 96, 128), F32),
    "gy": ((4, 96, 128), F32),
    "gsib": ((4, 96, 128), F32),
}
BLOCK = 8
UNROLL = 4


def step_kernel(int_ref, float_ref, feat_ref, cot_ref, tiles_ref, win_ref, wout_ref,
                out_ref, gin_ref, gout_ref, *scratch):
    w = types.SimpleNamespace(**dict(zip(SCRATCH, scratch)))
    send_sems, recv_sems, local_sems = scratch[len(SCRATCH):]
    chunks = SLOTS // CHUNK

    def chunk_copy(k):
        return pltpu.make_async_copy(tiles_ref.at[pl.ds(k * CHUNK, CHUNK)], w.buf.at[pl.ds(k * CHUNK, CHUNK)], local_sems.at[k])

    net = Net(send_sems, recv_sems)
    loads = [chunk_copy(k) for k in range(chunks)]
    own_x = pltpu.make_async_copy(feat_ref, w.xt.at[net.i], local_sems.at[chunks])
    own_c = pltpu.make_async_copy(
        cot_ref, w.cots.at[pl.ds(net.j * 2, 2)], local_sems.at[chunks + 1])
    own_x.start()
    own_c.start()
    for load in loads:
        load.start()
    w.sums_f[0] = jnp.zeros_like(w.sums_f[0])
    w.sums_a[0] = jnp.zeros_like(w.sums_a[0])
    net.barrier(("x", "core", "y", "z"))
    seen = {"x": 0, "cot": 0, 0: 0, 1: 0}
    done = {}

    def saw(name):
        seen[name] += 1

    def row_gather(name, src, ref_of, own_src, own_dst, level=0):
        for u, way in enumerate(WAYS):

            def ref(pos, u=u):
                return ref_of(pos * 2 + net.core, u)

            def have(pos, ref=ref):
                saw(name)
                net.spawn(arrive(net.send(ref(pos), ref(pos), "core"), lambda: saw(name)))

            ag_unit(net, "x", src(u), ref, have, way, level)
        net.spawn(arrive(net.send(own_src, own_dst, "core"), lambda: saw(name)))

    def halves(u):
        return pl.ds(u * 8, 8)

    row_gather("x", lambda u: feat_ref.at[halves(u), :], lambda i, u: w.xt.at[i, halves(u), :],
               feat_ref, w.xt.at[net.i])

    for part, (first, second) in enumerate((("y", "z"), ("z", "y"))):
        for u, way in enumerate(WAYS):
            rows = pl.ds(u * 64, 64)
            src = cot_ref.at[part, rows, :]

            def ref(pos1, pos2, rows=rows, first=first, part=part):
                block = pos1 + pos2 * 4 if first == "y" else pos1 * 4 + pos2
                return w.cots.at[2 * block + part, rows, :]

            def start_second(pos1, src=None, ref=ref, second=second, way=way):
                src = ref(pos1, net.at(second, 0)) if src is None else src
                ag_unit(net, second, src, lambda pos2: ref(pos1, pos2), lambda pos: saw("cot"), way, -1)

            def have_one(pos1, start_second=start_second):
                saw("cot")
                start_second(pos1)

            ag_unit(net, first, src, lambda pos1, ref=ref, second=second: ref(pos1, net.at(second, 0)),
                    have_one, way, level=-2)
            start_second(net.at(first, 0), src)

    def sums(base, k, lhs, product, store):
        def body(q, _):
            acc = None
            for v in range(UNROLL):
                n = base + q * UNROLL + v
                prev = store(n)[...] if acc is None else acc
                acc = prev * float_ref[k, n] + product(lhs[int_ref[k, n]], int_ref[k + 1, n])
                store(n + 1)[...] = acc
            return 0

        lax.fori_loop(0, BLOCK // UNROLL, body, 0)

    def pick(k, count, load, out):
        def body(r, _):
            out[r] = load(int_ref[k + 2, r])
            return 0

        lax.fori_loop(0, count, body, 0)

    def wide_product(values):
        def product(left, n):
            h, l = split(values[n])
            return dot16(left, jnp.concatenate([h, h], axis=0)) + dot16(left[:, :128], l)

        return product

    def narrow(left, h, l):
        pair = jnp.concatenate([h, l], axis=1)
        res = dot16(left, jnp.concatenate([pair, pair], axis=0))
        return res[:, :128] + res[:, 128:]

    def tiles():
        for k in range(chunks):
            loads[k].wait()

            def body(n, _, k=k):
                h, l = split(w.buf[k * CHUNK + n])
                w.acat[k * CHUNK + n] = jnp.concatenate([h, l], axis=1)
                return 0

            lax.fori_loop(0, CHUNK, body, 0)
            yield Tick(net, 0.5, 0)
        done["acat"] = True
        for k in range(chunks):

            def turn(n, _, k=k):
                t = k * CHUNK + n
                both = w.acat[t]
                w.atc[t] = jnp.concatenate([jnp.transpose(both[:, :128]), jnp.transpose(both[:, 128:])], axis=1)
                return 0

            lax.fori_loop(0, CHUNK, turn, 0)
            yield Tick(net, 0.6, 5)
        done["atc"] = True

    def first_layer():
        yield lambda: seen["x"] == 13 and done.get("acat")
        own_x.wait()

        def split_x(c, _):
            piece = w.xt[:, :, pl.ds(pl.multiple_of(c * 128, 128), 128)].reshape(128, 128)
            h, l = split(jnp.transpose(piece))
            w.xh[c] = h
            w.xl[c] = l
            return 0

        lax.fori_loop(0, 16, split_x, 0)
        yield Tick(net, 1.0, 0)
        for base in range(0, SLOTS, BLOCK):
            sums(base, 0, w.acat, lambda left, n: narrow(left, w.xh[n], w.xl[n]), lambda n: w.sums_f.at[n])
            yield Tick(net, 0.6, 0)
        pick(0, 32, lambda n: w.sums_f[n], w.fwd1)
        net.now += 0.5
        parts = []
        rs_plane(net, w.fwd1, w.a1, w.m1, w.b1, w.s, parts)
        yield lambda: len(parts) == 4
        pre = dot3(w.s[...], win_ref[...])
        hidden = pre * (1.0 / (1.0 + jnp.exp(-pre)))
        w.p[...] = pre
        w.h[...] = hidden
        for f in range(2):
            s2 = (w.s2_0, w.s2_1)[f]
            mine = s2.at[pl.ds(net.i * 2, 2)]
            mine[...] = dot3(hidden, wout_ref[:, f * 128 : f * 128 + 128]).reshape(2, 128, 128)
            net.now += 0.6
            row_gather(f, lambda u, s2=s2: s2.at[net.i * 2 + u], lambda i, u, s2=s2: s2.at[i * 2 + u], mine, mine, f)
            net.pump()
        done["pre"] = True
        for f in range(2):
            yield lambda: seen[f] == 13
            s2 = (w.s2_0, w.s2_1)[f]
            for base in range(0, SLOTS, BLOCK):
                sums(base, 0, w.acat, lambda left, n: narrow(left, *split(s2[n])), lambda n: w.sums_f.at[n])
                yield Tick(net, 0.6, 1)
            pick(0, 32, lambda n: w.sums_f[n], w.fwd2.at[f])
            net.now += 0.5
            rs_plane(net, w.fwd2.at[f], w.a2.at[f], w.m2.at[f], w.b2.at[f], out_ref, [],
                     slice(f * 128, f * 128 + 128), 6 * f)

    def adjoint():
        yield lambda: seen["cot"] == 60 and done.get("atc")
        own_c.wait()
        for base in range(0, SLOTS, BLOCK):
            sums(base, 3, w.atc, wide_product(w.cots), lambda n: w.sums_a.at[n])
            yield Tick(net, 0.9, 2)
        pick(3, 16, lambda n: w.sums_a[n], w.adj)
        net.now += 0.5
        parts = []
        for u, way in enumerate(WAYS):
            ready = {d: False for d in SHIFTS}
            for k, d in enumerate((2, way, -way, 0)):
                pos = net.at("x", d)

                def cores(u=u, k=k, d=d, pos=pos, ready=ready):
                    land = w.c3.at[u, k]
                    yield net.send(w.adj.at[(pos * 2 + 1 - net.core) * 2 + u], land, "core", 1, k)
                    w.m3[u, pos] = w.adj[(pos * 2 + net.core) * 2 + u] + land[...]
                    ready[d] = True

                net.spawn(cores())

            def emit_d(value, u=u):
                w.d[pl.ds(u * 128, 128), :] = value
                parts.append(u)

            rs_unit(net, "x", lambda pos, u=u: w.m3.at[u, pos], ready, lambda k, u=u: w.d3.at[u, k], emit_d, way, 0.5)
        yield lambda: len(parts) == 2 and done.get("pre")
        net.pump()
        d = w.d[...]
        pre = w.p[...]
        sg = 1.0 / (1.0 + jnp.exp(-pre))
        d_pre = dot3(d, wout_ref[...], (((1,), (1,)), ((), ()))) * sg * (1.0 + pre * (1.0 - sg))
        grad_in = dot3(jnp.transpose(w.s[...]), d_pre)
        grad_out = dot3(jnp.transpose(w.h[...]), d)
        for c in range(2):
            lanes = slice(c * 128, c * 128 + 128)
            w.g[c, pl.ds(0, 128), :] = grad_in[:, lanes]
            w.g[c, pl.ds(128, 256), :] = grad_out[:, lanes]
        net.now += 2.0
        yield net.send(w.g.at[1 - net.core], w.ge, "core", 1, 0)
        w.g1[...] = (w.g[net.core] + w.ge[...]).reshape(w.g1.shape)

        def total(terms, own, land):
            return (terms[own] + land[0]) + (land[1] + land[2])

        yield from reduce_direct(net, "x", w.g1, w.gf)
        w.gs[...] = total(w.g1, net.x, w.gf)
        for axis, land in (("y", w.g2), ("z", w.gz)):
            land[net.pos(axis)] = w.gs[...]
            yield from gather_direct(net, axis, land.at[net.pos(axis)], land)
            w.gs[...] = (land[0] + land[1]) + (land[2] + land[3])
        w.gy[net.x] = w.gs[...]
        yield from gather_direct(net, "x", w.gs, w.gy)
        yield net.send(w.gy, w.gsib, "core", 1, 0)
        mine, other = w.gy[...].reshape(384, 128), w.gsib[...].reshape(384, 128)
        first = net.core == 0
        low = jnp.where(first, mine, other)
        high = jnp.where(first, other, mine)
        gin_ref[:, :128] = low[:128]
        gin_ref[:, 128:] = high[:128]
        gout_ref[:, :128] = low[128:]
        gout_ref[:, 128:] = high[128:]

    net.spawn(tiles())
    net.spawn(first_layer())
    net.spawn(adjoint())
    net.run({64: w.acat, 128: w.sums_a})


def finish_kernel(a_ref, b_ref, c_ref, out_a, out_b, out_c):
    out_a[...] = a_ref[...]
    out_b[...] = b_ref[...]
    out_c[...] = c_ref[...]


ANY = pl.BlockSpec(memory_space=pl.ANY)
VM = pl.BlockSpec(memory_space=pltpu.VMEM)
SM = pl.BlockSpec(memory_space=pltpu.SMEM)


def shape(*dims, kind=F32):
    return jax.ShapeDtypeStruct(dims, kind)


def per_device(features, tile_rows, tile_cols, tile_values, weight_in, weight_out, cotangent):
    ints, floats = pl.pallas_call(
        tables_kernel,
        out_shape=(shape(8, 128, kind=jnp.int32), shape(8, 128)),
        in_specs=[VM, VM],
        out_specs=(VM, VM),
        scratch_shapes=[pltpu.VMEM((8, 128), jnp.int32)],
        name="tables",
    )(tile_rows.reshape(1, SLOTS), tile_cols.reshape(1, SLOTS))
    outs_shape = (shape(256, 256), shape(128, 256), shape(256, 256))
    outs = pl.pallas_call(
        step_kernel,
        out_shape=outs_shape,
        in_specs=[SM, SM, ANY, ANY, ANY, VM, VM],
        out_specs=(VM, VM, VM),
        scratch_shapes=[pltpu.VMEM(dims, kind) for dims, kind in SCRATCH.values()]
        + [
            pltpu.SemaphoreType.DMA((len(SIZES),)),
            pltpu.SemaphoreType.DMA((COPIES,)),
            pltpu.SemaphoreType.DMA((SLOTS // CHUNK + 2,)),
        ],
        compiler_params=pltpu.CompilerParams(
            collective_id=0, has_side_effects=True, vmem_limit_bytes=VMEM_LIMIT),
        name="step",
    )(ints, floats, features.T, cotangent.reshape(2, 128, 256), tile_values.reshape(SLOTS, 128, 128),
      weight_in, weight_out)
    return pl.pallas_call(
        finish_kernel, out_shape=outs_shape, in_specs=[VM] * 3, out_specs=(VM,) * 3, name="finish",
    )(*outs)


def solution(mesh):
    return jax.shard_map(
        per_device,
        mesh=mesh,
        in_specs=(
            P("col", "row"),
            P("row", "col", None),
            P("row", "col", None),
            P("row", "col", None, None, None),
            P(),
            P(),
            P(("col", "row"), None),
        ),
        out_specs=(P(("col", "row"), None), P(), P()),
        check_vma=False,
    )
```

```python
import heapq
import math
import types

import jax
import jax.numpy as jnp
from jax import lax
from jax.experimental import pallas as pl
from jax.experimental.pallas import tpu as pltpu
from jax.sharding import PartitionSpec as P

MESH = pl.DeviceIdType.MESH
F32 = jnp.float32
BF16 = jnp.bfloat16
VMEM_LIMIT = 67043328
CHUNK = 8
SLOTS = 80
TROWS = 32
TCOLS = 16
COPIES = 307
SIZES = tuple(k * 1024 for k in (32, 48, 64, 128, 192))


def split(v):
    hi = v.astype(BF16)
    return hi, (v - hi.astype(F32)).astype(BF16)


def dot16(a, b, dims=(((1,), (0,)), ((), ()))):
    return lax.dot_general(a, b, dims, preferred_element_type=F32)


def dot3(a, b, dims=(((1,), (0,)), ((), ()))):
    ah, al = split(a)
    bh, bl = split(b)
    return dot16(ah, bl, dims) + dot16(al, bh, dims) + dot16(ah, bh, dims)


class Copy:
    def __init__(self, src, dst, axis, shift):
        self.src, self.dst, self.axis, self.shift = src, dst, axis, shift
        self.bytes = 4 * math.prod(src.shape)
        self.copy = self.arrival = None


RATE = {"x": 45e3, "y": 45e3, "z": 45e3, "core": 250e3}
DELAY = {"x": 1.6, "y": 1.6, "z": 1.6, "core": 1.0}
WINDOW = 3.0


class Tick:
    def __init__(self, net, spent, level):
        net.now += spent
        self.arrival = net.now + level * 1e-3


class Net:
    def __init__(self, send_sems, recv_sems):
        self.send_sems, self.recv_sems = send_sems, recv_sems
        self.copies, self.sent = [], {}
        i, j = lax.axis_index("row"), lax.axis_index("col")
        self.x, self.core = i // 2, lax.rem(i, 2)
        self.z, self.y = j // 4, lax.rem(j, 4)
        self.i, self.j = i, j
        self.active, self.pending, self.free = [], {}, {}
        self.now, self.count = 0.0, 0

    def pos(self, axis):
        return {"x": self.x, "y": self.y, "z": self.z}[axis]

    def at(self, axis, shift):
        return lax.rem(self.pos(axis) + (shift + 4), 4)

    def peer(self, axis, shift):
        if axis == "core":
            return (self.x * 2 + 1 - self.core, self.j)
        p = self.at(axis, shift)
        if axis == "x":
            return (p * 2 + self.core, self.j)
        if axis == "y":
            return (self.i, self.z * 4 + p)
        return (self.i, p * 4 + self.y)

    def barrier(self, axes):
        sem = pltpu.get_barrier_semaphore()
        n = 0
        for axis in axes:
            for shift in (1,) if axis == "core" else (1, -1, 2):
                pl.semaphore_signal(sem, inc=1, device_id=self.peer(axis, shift), device_id_type=MESH)
                n += 1
        pl.semaphore_wait(sem, n)

    def send(self, src, dst, axis, shift=1, level=5):
        copy = Copy(src, dst, axis, shift)
        self.count += 1
        link = (axis, 1 if shift == 2 else shift)
        heapq.heappush(self.pending.setdefault(link, []), (level, self.count, copy))
        return copy

    def pump(self):
        for link, heap in self.pending.items():
            while heap and self.free.get(link, 0.0) < self.now + WINDOW:
                one = heapq.heappop(heap)[2]
                k = len(self.copies)
                one.copy = pltpu.make_async_remote_copy(
                    src_ref=one.src,
                    dst_ref=one.dst,
                    send_sem=self.send_sems.at[SIZES.index(one.bytes)],
                    recv_sem=self.recv_sems.at[k],
                    device_id=self.peer(one.axis, one.shift),
                    device_id_type=MESH,
                )
                one.copy.start()
                self.copies.append(one.copy)
                self.sent[one.bytes] = self.sent.get(one.bytes, 0) + one.bytes
                end = max(self.now, self.free.get(link, 0.0)) + one.bytes / RATE[one.axis]
                self.free[link] = end
                one.arrival = end + DELAY[one.axis] * (1.5 if one.shift == 2 else 1)

    def spawn(self, gen):
        self.active.append([gen, None])

    def run(self, whole):
        while True:
            moved = True
            while moved:
                moved = False
                for entry in list(self.active):
                    if entry[1] is None or (callable(entry[1]) and entry[1]()):
                        moved = True
                        self.step(entry)
            self.pump()
            waits = [e for e in self.active if not callable(e[1]) and e[1].arrival is not None]
            if waits:
                entry = min(waits, key=lambda e: e[1].arrival)
                self.now = max(self.now, entry[1].arrival)
                if isinstance(entry[1], Copy):
                    entry[1].copy.wait_recv()
                self.step(entry)
            elif any(self.pending.values()):
                self.now = min(self.free.get(link, 0.0) for link, heap in self.pending.items() if heap)
                self.now -= WINDOW / 2
            else:
                break
        assert not self.active
        assert len(self.copies) == COPIES
        for size, total in self.sent.items():
            unit = 128 if total % (128 * 1024) == 0 else 64
            span = whole[unit].at[pl.ds(0, total // (unit * 1024))]
            assert 4 * math.prod(span.shape) * (1 if unit == 128 else 0.5) == total
            pltpu.make_async_remote_copy(
                src_ref=span,
                dst_ref=span,
                send_sem=self.send_sems.at[SIZES.index(size)],
                recv_sem=self.recv_sems.at[0],
                device_id=self.peer("core", 1),
                device_id_type=MESH,
            ).wait_send()

    def step(self, entry):
        try:
            entry[1] = next(entry[0])
        except StopIteration:
            self.active.remove(entry)


def arrive(copy, have=None):
    yield copy
    if have is not None:
        have()


def ag_unit(net, axis, src, ref, have, way, level=5):
    p = net.at(axis, 0)
    near = net.send(src, ref(p), axis, way, level)
    other = net.send(src, ref(p), axis, -way, level)

    def chain():
        yield near
        pos = net.at(axis, -way)
        onward = net.send(ref(pos), ref(pos), axis, way, level)
        have(pos)
        yield onward
        have(net.at(axis, 2))

    net.spawn(chain())
    net.spawn(arrive(other, lambda: have(net.at(axis, way))))


def rs_unit(net, axis, part, ready, stage, emit, way, level=5, after=None):
    r, m, q = (stage(k) for k in range(3))
    box = []
    after = level if after is None else after

    def near():
        yield lambda: ready[-way]
        box.append(net.send(part(net.at(axis, -way)), q, axis, -way, level))

    def far():
        yield lambda: ready[2]
        first = net.send(part(net.at(axis, 2)), r, axis, way, level)
        yield first
        yield lambda: ready[way]
        r[...] = r[...] + part(net.at(axis, way))[...]
        yield net.send(r, m, axis, way, after)
        yield lambda: box
        yield box[0]
        yield lambda: ready[0]
        emit(part(net.at(axis, 0))[...] + (m[...] + q[...]))

    net.spawn(far())
    net.spawn(near())


def gather_direct(net, axis, src, dst, level=0):
    copies = [net.send(src, dst.at[net.at(axis, 0)], axis, d, level) for d in (2, 1, -1)]
    for copy in copies[1:] + copies[:1]:
        yield copy


def reduce_direct(net, axis, terms, land, level=0):
    copies = [net.send(terms.at[net.at(axis, d)], land.at[k], axis, d, level) for k, d in enumerate((2, 1, -1))]
    for copy in copies[1:] + copies[:1]:
        yield copy


ALL = {0: True, 1: True, 2: True, -1: True}
SHIFTS = (2, 1, -1, 0)
WAYS = (1, -1)


def rs_plane(net, tiles, stage_one, middle, stage_two, out, done, lanes=slice(None), base=0):
    for part, (first, second) in enumerate((("z", "y"), ("y", "z"))):
        for u, way in enumerate(WAYS):
            ready = {d: False for d in SHIFTS}
            for k, d in enumerate((2, way, -way, 0)):
                pos2 = net.at(second, d)

                def term(pos1, pos2=pos2, part=part, u=u, first=first):
                    block = pos1 * 4 + pos2 if first == "z" else pos2 * 4 + pos1
                    return tiles.at[2 * block + part, pl.ds(u * 64, 64), :]

                def land(s, part=part, u=u, k=k):
                    return stage_one.at[part, k, u, s]

                def emit(value, part=part, u=u, pos2=pos2, d=d, ready=ready):
                    middle[part, pos2, u] = value
                    ready[d] = True

                rs_unit(net, first, term, ALL, land, emit, way, level=base + 3 + k, after=base + 2)

            def term2(pos, part=part, u=u):
                return middle.at[part, pos, u]

            def land2(s, part=part, u=u):
                return stage_two.at[part, u, s]

            def emit2(value, part=part, u=u):
                out[part * 128 + u * 64 : part * 128 + u * 64 + 64, lanes] = value
                done.append((part, u))

            rs_unit(net, second, term2, ready, land2, emit2, way, level=base + 1)


def tables_kernel(rows_ref, cols_ref, int_ref, float_ref, pad):
    pad[0:1, :] = jnp.full((1, 128), TROWS, jnp.int32)
    pad[1:2, :] = jnp.zeros((1, 128), jnp.int32)
    pad[0:1, :SLOTS] = rows_ref[...]
    pad[1:2, :SLOTS] = cols_ref[...]
    lane = lax.broadcasted_iota(jnp.int32, (128, 128), 1)
    line = lax.broadcasted_iota(jnp.int32, (128, 128), 0)

    def wide(v):
        return jnp.broadcast_to(v, (128, 128))

    def count(v):
        return jnp.sum(v, axis=0, keepdims=True)

    row, col = pad[0:1, :], pad[1:2, :]
    used = row < TROWS
    for major, minor, size, k in ((row, col, TROWS, 0), (col, row, TCOLS, 3)):
        major, minor = jnp.where(used, major, size), jnp.where(used, minor, 0)
        key = wide(major * 64 + minor)
        key_t = jnp.transpose(key)
        before = (key_t < key) | ((key_t == key) & (line < lane))
        rank_t = jnp.transpose(wide(count(before.astype(jnp.int32))))
        here = rank_t == lane
        order = count(jnp.where(here, line, 0))
        sorted_key = count(jnp.where(here, key_t, 0))
        group = sorted_key // 64
        group_t = jnp.transpose(wide(group))
        found = count((group_t == lane).astype(jnp.int32)) > 0
        last = jnp.where(found, count((group_t <= lane).astype(jnp.int32)), 0)
        int_ref[k : k + 1, :] = order
        int_ref[k + 1 : k + 2, :] = sorted_key - group * 64
        int_ref[k + 2 : k + 3, :] = last
        same = count(((group_t == wide(group)) & (line + 1 == lane)).astype(jnp.int32))
        float_ref[k : k + 1, :] = same.astype(F32)


SCRATCH = {
    "buf": ((SLOTS, 128, 128), F32),
    "acat": ((SLOTS, 128, 256), BF16),
    "atc": ((SLOTS, 128, 256), BF16),
    "sums_f": ((SLOTS + 1, 128, 128), F32),
    "sums_a": ((SLOTS + 1, 128, 256), F32),
    "xt": ((8, 16, 2048), F32),
    "xh": ((16, 128, 128), BF16),
    "xl": ((16, 128, 128), BF16),
    "cots": ((32, 128, 256), F32),
    "s2_0": ((16, 128, 128), F32),
    "s2_1": ((16, 128, 128), F32),
    "fwd1": ((32, 128, 128), F32),
    "fwd2": ((2, 32, 128, 128), F32),
    "adj": ((16, 128, 256), F32),
    "a1": ((2, 4, 2, 3, 64, 128), F32),
    "m1": ((2, 4, 2, 64, 128), F32),
    "b1": ((2, 2, 3, 64, 128), F32),
    "a2": ((2, 2, 4, 2, 3, 64, 128), F32),
    "m2": ((2, 2, 4, 2, 64, 128), F32),
    "b2": ((2, 2, 2, 3, 64, 128), F32),
    "c3": ((2, 4, 128, 256), F32),
    "m3": ((2, 4, 128, 256), F32),
    "d3": ((2, 3, 128, 256), F32),
    "win": ((128, 256), F32),
    "wout": ((256, 256), F32),
    "s": ((256, 128), F32),
    "d": ((256, 256), F32),
    "h": ((256, 256), F32),
    "p": ((256, 256), F32),
    "g": ((2, 384, 128), F32),
    "ge": ((384, 128), F32),
    "g1": ((4, 96, 128), F32),
    "gf": ((3, 96, 128), F32),
    "gs": ((96, 128), F32),
    "g2": ((4, 96, 128), F32),
    "gz": ((4, 96, 128), F32),
    "gy": ((4, 96, 128), F32),
    "gsib": ((4, 96, 128), F32),
}
BLOCK = 4
UNROLL = 4


def step_kernel(int_ref, float_ref, feat_ref, cot_ref, tiles_ref, win_ref, wout_ref,
                out_ref, gin_ref, gout_ref, *scratch):
    w = types.SimpleNamespace(**dict(zip(SCRATCH, scratch)))
    send_sems, recv_sems, local_sems = scratch[len(SCRATCH):]
    chunks = SLOTS // CHUNK

    def chunk_copy(k):
        return pltpu.make_async_copy(tiles_ref.at[pl.ds(k * CHUNK, CHUNK)], w.buf.at[pl.ds(k * CHUNK, CHUNK)], local_sems.at[k])

    net = Net(send_sems, recv_sems)
    loads = [chunk_copy(k) for k in range(chunks)]
    own_x = pltpu.make_async_copy(feat_ref, w.xt.at[net.i], local_sems.at[chunks])
    own_c = pltpu.make_async_copy(
        cot_ref, w.cots.at[pl.ds(net.j * 2, 2)], local_sems.at[chunks + 1])
    weights = [
        pltpu.make_async_copy(win_ref, w.win, local_sems.at[chunks + 2]),
        pltpu.make_async_copy(wout_ref, w.wout, local_sems.at[chunks + 3]),
    ]
    for weight in weights:
        weight.start()
    own_x.start()
    own_c.start()
    for load in loads:
        load.start()
    w.sums_f[0] = jnp.zeros_like(w.sums_f[0])
    w.sums_a[0] = jnp.zeros_like(w.sums_a[0])
    net.barrier(("x", "core", "y", "z"))
    seen = {"x": 0, "cot": 0, 0: 0, 1: 0}
    done = {}

    def saw(name):
        seen[name] += 1

    def row_gather(name, src, ref_of, own_src, own_dst, level=0):
        for u, way in enumerate(WAYS):

            def ref(pos, u=u):
                return ref_of(pos * 2 + net.core, u)

            def have(pos, ref=ref):
                saw(name)
                net.spawn(arrive(net.send(ref(pos), ref(pos), "core"), lambda: saw(name)))

            ag_unit(net, "x", src(u), ref, have, way, level)
        net.spawn(arrive(net.send(own_src, own_dst, "core"), lambda: saw(name)))

    def halves(u):
        return pl.ds(u * 8, 8)

    row_gather("x", lambda u: feat_ref.at[halves(u), :], lambda i, u: w.xt.at[i, halves(u), :],
               feat_ref, w.xt.at[net.i])

    for part, (first, second) in enumerate((("y", "z"), ("z", "y"))):
        for u, way in enumerate(WAYS):
            rows = pl.ds(u * 64, 64)
            src = cot_ref.at[part, rows, :]

            def ref(pos1, pos2, rows=rows, first=first, part=part):
                block = pos1 + pos2 * 4 if first == "y" else pos1 * 4 + pos2
                return w.cots.at[2 * block + part, rows, :]

            def start_second(pos1, src=None, ref=ref, second=second, way=way):
                src = ref(pos1, net.at(second, 0)) if src is None else src
                ag_unit(net, second, src, lambda pos2: ref(pos1, pos2), lambda pos: saw("cot"), way, -1)

            def have_one(pos1, start_second=start_second):
                saw("cot")
                start_second(pos1)

            ag_unit(net, first, src, lambda pos1, ref=ref, second=second: ref(pos1, net.at(second, 0)),
                    have_one, way, level=-2)
            start_second(net.at(first, 0), src)

    def sums(base, k, lhs, product, store):
        def body(q, _):
            acc = None
            for v in range(UNROLL):
                n = base + q * UNROLL + v
                prev = store(n)[...] if acc is None else acc
                acc = prev * float_ref[k, n] + product(lhs[int_ref[k, n]], int_ref[k + 1, n])
                store(n + 1)[...] = acc
            return 0

        lax.fori_loop(0, BLOCK // UNROLL, body, 0)

    def pick(k, count, load, out):
        def body(r, _):
            out[r] = load(int_ref[k + 2, r])
            return 0

        lax.fori_loop(0, count, body, 0)

    def wide_product(values):
        def product(left, n):
            h, l = split(values[n])
            return dot16(left, jnp.concatenate([h, h], axis=0)) + dot16(left[:, :128], l)

        return product

    def narrow(left, h, l):
        pair = jnp.concatenate([h, l], axis=1)
        res = dot16(left, jnp.concatenate([pair, pair], axis=0))
        return res[:, :128] + res[:, 128:]

    def tiles():
        for k in range(chunks):
            loads[k].wait()

            def body(n, _, k=k):
                h, l = split(w.buf[k * CHUNK + n])
                w.acat[k * CHUNK + n] = jnp.concatenate([h, l], axis=1)
                return 0

            lax.fori_loop(0, CHUNK, body, 0)
            yield Tick(net, 0.5, 0)
        done["acat"] = True
        for k in range(chunks):

            def turn(n, _, k=k):
                t = k * CHUNK + n
                both = w.acat[t]
                w.atc[t] = jnp.concatenate([jnp.transpose(both[:, :128]), jnp.transpose(both[:, 128:])], axis=1)
                return 0

            lax.fori_loop(0, CHUNK, turn, 0)
            yield Tick(net, 0.6, 5)
        done["atc"] = True

    def first_layer():
        yield lambda: seen["x"] == 13 and done.get("acat")
        own_x.wait()

        def split_x(c, _):
            piece = w.xt[:, :, pl.ds(pl.multiple_of(c * 128, 128), 128)].reshape(128, 128)
            h, l = split(jnp.transpose(piece))
            w.xh[c] = h
            w.xl[c] = l
            return 0

        lax.fori_loop(0, 16, split_x, 0)
        yield Tick(net, 1.0, 0)
        for base in range(0, SLOTS, BLOCK):
            sums(base, 0, w.acat, lambda left, n: narrow(left, w.xh[n], w.xl[n]), lambda n: w.sums_f.at[n])
            yield Tick(net, 0.3, 0)
        pick(0, 32, lambda n: w.sums_f[n], w.fwd1)
        net.now += 0.5
        parts = []
        rs_plane(net, w.fwd1, w.a1, w.m1, w.b1, w.s, parts)
        yield lambda: len(parts) == 4
        for weight in weights:
            weight.wait()
        pre = dot3(w.s[...], w.win[...])
        hidden = pre * (1.0 / (1.0 + jnp.exp(-pre)))
        w.p[...] = pre
        w.h[...] = hidden
        for f in range(2):
            s2 = (w.s2_0, w.s2_1)[f]
            mine = s2.at[pl.ds(net.i * 2, 2)]
            mine[...] = dot3(hidden, w.wout[:, f * 128 : f * 128 + 128]).reshape(2, 128, 128)
            net.now += 0.6
            row_gather(f, lambda u, s2=s2: s2.at[net.i * 2 + u], lambda i, u, s2=s2: s2.at[i * 2 + u], mine, mine, f)
            net.pump()
        done["pre"] = True
        for f in range(2):
            yield lambda: seen[f] == 13
            s2 = (w.s2_0, w.s2_1)[f]
            for base in range(0, SLOTS, BLOCK):
                sums(base, 0, w.acat, lambda left, n: narrow(left, *split(s2[n])), lambda n: w.sums_f.at[n])
                yield Tick(net, 0.3, 1)
            pick(0, 32, lambda n: w.sums_f[n], w.fwd2.at[f])
            net.now += 0.5
            rs_plane(net, w.fwd2.at[f], w.a2.at[f], w.m2.at[f], w.b2.at[f], out_ref, [],
                     slice(f * 128, f * 128 + 128), 6 * f)

    def adjoint():
        yield lambda: seen["cot"] == 60 and done.get("atc")
        own_c.wait()
        for base in range(0, SLOTS, BLOCK):
            sums(base, 3, w.atc, wide_product(w.cots), lambda n: w.sums_a.at[n])
            yield Tick(net, 0.45, 2)
        pick(3, 16, lambda n: w.sums_a[n], w.adj)
        net.now += 0.5
        parts = []
        for u, way in enumerate(WAYS):
            ready = {d: False for d in SHIFTS}
            for k, d in enumerate((2, way, -way, 0)):
                pos = net.at("x", d)

                def cores(u=u, k=k, d=d, pos=pos, ready=ready):
                    land = w.c3.at[u, k]
                    yield net.send(w.adj.at[(pos * 2 + 1 - net.core) * 2 + u], land, "core", 1, k)
                    w.m3[u, pos] = w.adj[(pos * 2 + net.core) * 2 + u] + land[...]
                    ready[d] = True

                net.spawn(cores())

            def emit_d(value, u=u):
                w.d[pl.ds(u * 128, 128), :] = value
                parts.append(u)

            rs_unit(net, "x", lambda pos, u=u: w.m3.at[u, pos], ready, lambda k, u=u: w.d3.at[u, k], emit_d, way, 0.5)
        yield lambda: len(parts) == 2 and done.get("pre")
        net.pump()
        d = w.d[...]
        pre = w.p[...]
        sg = 1.0 / (1.0 + jnp.exp(-pre))
        d_pre = dot3(d, w.wout[...], (((1,), (1,)), ((), ()))) * sg * (1.0 + pre * (1.0 - sg))
        grad_in = dot3(jnp.transpose(w.s[...]), d_pre)
        grad_out = dot3(jnp.transpose(w.h[...]), d)
        for c in range(2):
            lanes = slice(c * 128, c * 128 + 128)
            w.g[c, pl.ds(0, 128), :] = grad_in[:, lanes]
            w.g[c, pl.ds(128, 256), :] = grad_out[:, lanes]
        net.now += 2.0
        yield net.send(w.g.at[1 - net.core], w.ge, "core", 1, 0)
        w.g1[...] = (w.g[net.core] + w.ge[...]).reshape(w.g1.shape)

        def total(terms, own, land):
            return (terms[own] + land[0]) + (land[1] + land[2])

        yield from reduce_direct(net, "x", w.g1, w.gf)
        w.gs[...] = total(w.g1, net.x, w.gf)
        for axis, land in (("y", w.g2), ("z", w.gz)):
            land[net.pos(axis)] = w.gs[...]
            yield from gather_direct(net, axis, land.at[net.pos(axis)], land)
            w.gs[...] = (land[0] + land[1]) + (land[2] + land[3])
        w.gy[net.x] = w.gs[...]
        yield from gather_direct(net, "x", w.gs, w.gy)
        yield net.send(w.gy, w.gsib, "core", 1, 0)
        mine, other = w.gy[...].reshape(384, 128), w.gsib[...].reshape(384, 128)
        first = net.core == 0
        low = jnp.where(first, mine, other)
        high = jnp.where(first, other, mine)
        gin_ref[:, :128] = low[:128]
        gin_ref[:, 128:] = high[:128]
        gout_ref[:, :128] = low[128:]
        gout_ref[:, 128:] = high[128:]

    net.spawn(tiles())
    net.spawn(first_layer())
    net.spawn(adjoint())
    net.run({64: w.acat, 128: w.sums_a})


def finish_kernel(a_ref, b_ref, c_ref, out_a, out_b, out_c):
    out_a[...] = a_ref[...]
    out_b[...] = b_ref[...]
    out_c[...] = c_ref[...]


ANY = pl.BlockSpec(memory_space=pl.ANY)
VM = pl.BlockSpec(memory_space=pltpu.VMEM)
SM = pl.BlockSpec(memory_space=pltpu.SMEM)


def shape(*dims, kind=F32):
    return jax.ShapeDtypeStruct(dims, kind)


def per_device(features, tile_rows, tile_cols, tile_values, weight_in, weight_out, cotangent):
    ints, floats = pl.pallas_call(
        tables_kernel,
        out_shape=(shape(8, 128, kind=jnp.int32), shape(8, 128)),
        in_specs=[VM, VM],
        out_specs=(VM, VM),
        scratch_shapes=[pltpu.VMEM((8, 128), jnp.int32)],
        name="tables",
    )(tile_rows.reshape(1, SLOTS), tile_cols.reshape(1, SLOTS))
    outs_shape = (shape(256, 256), shape(128, 256), shape(256, 256))
    outs = pl.pallas_call(
        step_kernel,
        out_shape=outs_shape,
        in_specs=[SM, SM, ANY, ANY, ANY, ANY, ANY],
        out_specs=(VM, VM, VM),
        scratch_shapes=[pltpu.VMEM(dims, kind) for dims, kind in SCRATCH.values()]
        + [
            pltpu.SemaphoreType.DMA((len(SIZES),)),
            pltpu.SemaphoreType.DMA((COPIES,)),
            pltpu.SemaphoreType.DMA((SLOTS // CHUNK + 4,)),
        ],
        compiler_params=pltpu.CompilerParams(
            collective_id=0, has_side_effects=True, vmem_limit_bytes=VMEM_LIMIT),
        name="step",
    )(ints, floats, features.T, cotangent.reshape(2, 128, 256), tile_values.reshape(SLOTS, 128, 128),
      weight_in, weight_out)
    return pl.pallas_call(
        finish_kernel, out_shape=outs_shape, in_specs=[VM] * 3, out_specs=(VM,) * 3, name="finish",
    )(*outs)


def solution(mesh):
    return jax.shard_map(
        per_device,
        mesh=mesh,
        in_specs=(
            P("col", "row"),
            P("row", "col", None),
            P("row", "col", None),
            P("row", "col", None, None, None),
            P(),
            P(),
            P(("col", "row"), None),
        ),
        out_specs=(P(("col", "row"), None), P(), P()),
        check_vma=False,
    )
```
